256 devices in a mesh: row: 64 (over x, z_lo, y, core), col: 4 (over z_hi).
Axes of the slice: x: 4, y: 4, z: 8 (z_hi: 4, z_lo: 2; z = z_hi * 2 + z_lo), core: 2. Of those that a mesh axis runs over, the one named last changes fastest.
Arguments:
- fields: float32 [4, 128, 512, 512], P(None, 'row', None, 'col'), may hold values from -6 to 6
- diffusivity: float32 [4], replicated, may hold values from 0.05 to 0.3
- records: float32 [6, 2097152], P(None, ('row', 'col')), may hold values from -6 to 6
- response_time: float32 [2097152], P(('row', 'col')), may hold values from 0.5 to 4
- cell_index: int32 [2097152], P(('row', 'col')), may hold values from 0 to 131071
- counts: int32 [256], P(('row', 'col')), may hold values from 4096 to 8192, as said below
- destination: int32 [2097152], P(('row', 'col')), may hold values from 0 to 4, as said below
- slot: int32 [2097152], P(('row', 'col')), may hold values from 0 to 255, as said below
Outputs:
- tendency: float32 [4, 128, 512, 512], P(None, 'row', None, 'col')
- kept: float32 [6, 2097152], P(None, ('row', 'col'))
- arrivals: float32 [4, 6, 65536], P(None, None, ('row', 'col'))
The draws below stay inside these ranges and needn't reach their ends.
Inputs may be any that keep to these rules, and one draw needn't show every extreme that they name: `counts`: both wall rows of pencils are full. `destination`: only live particles leave; none leaves row index 0 downward or row index 63 upward. For each pencil and direction the leaving particles' slots are distinct; pencil 0 sends exactly 256 particles toward col index + 1; slot is 0 for particles that stay.
All inputs are finite; a program needn't handle non-finite values.
Results may differ from the reference program's by a relative error of at most 0.00009.
Values sent between devices are 32-bit elements; how exact they have to be, the bound alone decides.
A program may use at most 192 MiB of HBM per device.

```python
import math
import jax
import jax.numpy as jnp
from jax import lax

YR = 2
ZC = 128
NX = 512
NY = 128
NZ = 512
PART_DEV = 8192
MIG = 256
PENCIL_ROWS = 64
PENCIL_COLS = 4
PARTICLES = 2097152


def pencil_lists(key):
    pencils = PENCIL_ROWS * PENCIL_COLS
    keys = jax.random.split(jax.random.fold_in(key, 7), 3)
    rows_of = jnp.arange(pencils, dtype=jnp.int32) // PENCIL_COLS
    middle_row = (PENCIL_ROWS - 1) // 2
    gap_scale = max(middle_row, 1)
    wall_gap = jnp.minimum(jnp.minimum(rows_of, PENCIL_ROWS - 1 - rows_of), gap_scale)
    reduction = jax.random.randint(keys[0], (pencils,), 0, PART_DEV // 2 + 1, dtype=jnp.int32)
    reduction = reduction.at[middle_row * PENCIL_COLS].set(PART_DEV // 2)
    live_count = (PART_DEV - reduction * wall_gap // gap_scale).astype(jnp.int32)
    leave = jax.random.randint(keys[1], (pencils, 4), MIG // 3, MIG + 1, dtype=jnp.int32)
    leave = leave.at[:, 0].set(jnp.where(rows_of == PENCIL_ROWS - 1, 0, leave[:, 0]))
    leave = leave.at[:, 1].set(jnp.where(rows_of == 0, 0, leave[:, 1]))
    leave = leave.at[0, 2].set(MIG)
    orders = jax.vmap(lambda one_key: jax.random.permutation(one_key, PART_DEV))(jax.random.split(keys[2], pencils))
    orders = orders.astype(jnp.int32)
    local = jnp.arange(PART_DEV, dtype=jnp.int32)
    scores = jnp.where(local[None, :] < live_count[:, None], orders, orders + PART_DEV)
    ranking = jnp.argsort(jnp.argsort(scores, axis=1), axis=1).astype(jnp.int32)
    bounds = jnp.cumsum(leave, axis=1).astype(jnp.int32)
    group = jnp.sum((ranking[:, :, None] >= bounds[:, None, :]).astype(jnp.int32), axis=2).astype(jnp.int32)
    starts = bounds - leave
    first_slot = jnp.take_along_axis(starts, jnp.minimum(group, 3), axis=1)
    target = jnp.where(group < 4, group + 1, 0).astype(jnp.int32)
    place = jnp.where(group < 4, ranking - first_slot, 0).astype(jnp.int32)
    return (live_count, target.reshape(-1), place.reshape(-1))


def draw_counts(key, part):
    return pencil_lists(key)[0]


def draw_destination(key, part):
    return pencil_lists(key)[1]


def draw_slot(key, part):
    return pencil_lists(key)[2]


def place_ends(result, key, least, largest):
    spot = [jax.random.randint(jax.random.fold_in(key, axis), (), 0, length) for axis, length in enumerate(result.shape)]
    main_axis = result.shape.index(max(result.shape))
    beside = spot[:main_axis] + [(spot[main_axis] + 1) % result.shape[main_axis]] + spot[main_axis + 1:]
    return result.at[tuple(spot)].set(least).at[tuple(beside)].set(largest)


def block_scale(key, shape, pieces, least, high):
    loudness, own = 1.0, jax.random.fold_in(key, 6)
    for dim, shards_of in pieces:
        draws = jnp.exp(jax.random.uniform(jax.random.fold_in(own, dim), (shards_of,), jnp.float32, least / len(pieces), high / len(pieces)))
        loudness = loudness * jnp.repeat(draws, shape[dim] // shards_of).reshape([-1 if axis == dim else 1 for axis in range(len(shape))])
    return loudness


def bell_draw(key, shape, width, reach, shards=(), held_as=jnp.bfloat16):
    values = width * jax.random.normal(key, shape, jnp.float32)
    if shards:
        values = values * block_scale(key, shape, shards, -0.22, 0.18)
    return jnp.clip(values, -reach, reach).astype(held_as)


def setup_inputs(seed: int = 0) -> dict:
    key_of = jax.random.split(jax.random.key(seed), 9)
    return {
        "fields": bell_draw(key_of[0], (4, NY, NX, NZ), 1.0, 6.0, ((1, 64), (3, 4)), jnp.float32),
        "diffusivity": jnp.clip(jnp.exp(jax.random.uniform(key_of[1], (4,), jnp.float32, math.log(0.05), math.log(0.3))), 0.05, 0.3),
        "records": bell_draw(key_of[2], (6, PARTICLES), 1.0, 6.0, ((1, 256),), jnp.float32),
        "response_time": jnp.clip(jnp.exp(math.log(4.0) - 2.0794415 * jax.random.uniform(key_of[3], (PARTICLES,), jnp.float32) ** block_scale(key_of[3], (PARTICLES,), ((0, 256),), -0.2, 0.2)), 0.5, 4.0),
        "cell_index": place_ends(jax.random.randint(key_of[4], (PARTICLES,), 0, NX * YR * ZC), jax.random.fold_in(key_of[4], 1), 0, (NX * YR * ZC) - 1).astype(jnp.int32),
        "counts": draw_counts(jax.random.fold_in(key_of[8], 71), 0),
        "destination": draw_destination(jax.random.fold_in(key_of[8], 71), 0),
        "slot": draw_slot(jax.random.fold_in(key_of[8], 71), 0),
    }


time_step = 0.2
coupling = 0.5
stretch = 1.5

def periodic_compact(points):
    index = jnp.arange(points, dtype=jnp.int32)
    offset = (index[None, :] - index[:, None]) % points
    lhs = jnp.where(offset == 0, 1.0, 0.0) + jnp.where((offset == 1) | (offset == points - 1), 1.0 / 3.0, 0.0)
    rhs = jnp.where(offset == 1, 7.0 / 9.0, 0.0) - jnp.where(offset == points - 1, 7.0 / 9.0, 0.0)
    rhs = rhs + jnp.where(offset == 2, 1.0 / 36.0, 0.0) - jnp.where(offset == points - 2, 1.0 / 36.0, 0.0)
    factor = jnp.linalg.cholesky(lhs.astype(jnp.float32))
    return jax.scipy.linalg.cho_solve((factor, True), rhs.astype(jnp.float32))

def wall_compact(points):
    index = jnp.arange(points, dtype=jnp.int32)
    first = index == 0
    final = index == points - 1
    near = (index == 1) | (index == points - 2)
    lower = jnp.where(first, 0.0, jnp.where(final, 2.0, jnp.where(near, 0.25, 1.0 / 3.0))).astype(jnp.float32)
    upper = jnp.where(final, 0.0, jnp.where(first, 2.0, jnp.where(near, 0.25, 1.0 / 3.0))).astype(jnp.float32)
    middle = jnp.ones((points,), jnp.float32)
    offset = index[None, :] - index[:, None]
    inner = jnp.where(offset == 1, 7.0 / 9.0, 0.0) - jnp.where(offset == -1, 7.0 / 9.0, 0.0)
    inner = inner + jnp.where(offset == 2, 1.0 / 36.0, 0.0) - jnp.where(offset == -2, 1.0 / 36.0, 0.0)
    padde_rows = jnp.where(offset == 1, 0.75, 0.0) - jnp.where(offset == -1, 0.75, 0.0)
    top_row = jnp.where(offset == 0, -2.5, 0.0) + jnp.where(offset == 1, 2.0, 0.0) + jnp.where(offset == 2, 0.5, 0.0)
    end_row = jnp.where(offset == 0, 2.5, 0.0) - jnp.where(offset == -1, 2.0, 0.0) - jnp.where(offset == -2, 0.5, 0.0)
    rhs = jnp.where(first[:, None], top_row, jnp.where(final[:, None], end_row, jnp.where(near[:, None], padde_rows, inner)))
    solved = lax.linalg.tridiagonal_solve(lower, middle, upper, rhs.astype(jnp.float32))
    coord = -1.0 + 2.0 * index.astype(jnp.float32) / (points - 1)
    slope = stretch * (1.0 - jnp.tanh(stretch * coord) ** 2) / math.tanh(stretch)
    return solved / slope[:, None]

def spectral_matrix(points):
    index = jnp.arange(points, dtype=jnp.int32)
    offset = index[:, None] - index[None, :]
    parity = (1 - 2 * (offset % 2)).astype(jnp.float32)
    angle = math.pi * offset.astype(jnp.float32) / points
    safe_angle = jnp.where(offset == 0, 1.0, angle)
    value = math.pi / points * parity * jnp.cos(safe_angle) / jnp.sin(safe_angle)
    return jnp.where(offset == 0, 0.0, value).astype(jnp.float32)

def reference(fields, diffusivity, records, response_time, cell_index, counts, destination, slot):
    highest = lax.Precision.HIGHEST
    deriv_x = periodic_compact(NX)
    deriv_y = wall_compact(NY)
    deriv_z = spectral_matrix(NZ)
    second_x = jnp.dot(deriv_x, deriv_x, precision=highest)
    second_y = jnp.dot(deriv_y, deriv_y, precision=highest)
    second_z = jnp.dot(deriv_z, deriv_z, precision=highest)
    speed_u = fields[0]
    speed_v = fields[1]
    speed_w = fields[2]

    def component_tendency(operands):
        field, viscous = operands
        along_x = jnp.einsum('ij,yjz->yiz', deriv_x, field, precision=highest)
        curve_x = jnp.einsum('ij,yjz->yiz', second_x, field, precision=highest)
        along_y = jnp.einsum('ij,jxz->ixz', deriv_y, field, precision=highest)
        curve_y = jnp.einsum('ij,jxz->ixz', second_y, field, precision=highest)
        along_z = jnp.einsum('ij,yxj->yxi', deriv_z, field, precision=highest)
        curve_z = jnp.einsum('ij,yxj->yxi', second_z, field, precision=highest)
        partial_x = -speed_u * along_x + viscous * curve_x
        partial_y = -speed_v * along_y + viscous * curve_y
        partial_z = -speed_w * along_z + viscous * curve_z
        return partial_x + partial_y + partial_z
    summed = lax.map(component_tendency, (fields, diffusivity))
    pencils = PENCIL_ROWS * PENCIL_COLS
    total_slots = PART_DEV * pencils
    position = jnp.arange(total_slots, dtype=jnp.int32)
    pencil = position // PART_DEV
    local = position % PART_DEV
    pencil_row = pencil // PENCIL_COLS
    pencil_col = pencil % PENCIL_COLS
    plane_y = pencil_row * YR + cell_index // (NX * ZC)
    plane_x = cell_index // ZC % NX
    plane_z = pencil_col * ZC + cell_index % ZC
    live = local < counts[pencil]
    fluid = fields[0:3][:, plane_y, plane_x, plane_z]
    drag = (fluid - records[3:6]) / response_time
    velocity = records[3:6] + time_step * drag
    moved_pos = records[0:3] + time_step * velocity
    moved = jnp.concatenate([moved_pos, velocity], axis=0)
    force = jnp.where(live[None, :], -coupling * drag, 0.0)
    deposit = jnp.zeros((3, NY, NX, NZ), jnp.float32).at[:, plane_y, plane_x, plane_z].add(force)
    tendency = summed.at[0:3].add(deposit)
    staying = live & (destination == 0)
    kept = jnp.where(staying[None, :], moved, 0.0)
    leaving = live & (destination > 0)
    target = jnp.where(leaving, pencil * (4 * MIG) + (destination - 1) * MIG + slot, pencils * 4 * MIG)
    outgoing = jnp.zeros((6, pencils * 4 * MIG + 1), jnp.float32).at[:, target].add(jnp.where(leaving[None, :], moved, 0.0))
    outgoing = outgoing[:, :-1].reshape(6, PENCIL_ROWS, PENCIL_COLS, 4, MIG)
    from_lower = jnp.pad(outgoing[:, :-1, :, 0], ((0, 0), (1, 0), (0, 0), (0, 0)))
    from_upper = jnp.pad(outgoing[:, 1:, :, 1], ((0, 0), (0, 1), (0, 0), (0, 0)))
    from_left = jnp.roll(outgoing[:, :, :, 2], 1, axis=2)
    from_right = jnp.roll(outgoing[:, :, :, 3], -1, axis=2)
    arrivals = jnp.stack([from_lower, from_upper, from_left, from_right], axis=0)
    arrivals = arrivals.reshape(4, 6, pencils * MIG)
    return (tendency, kept, arrivals)
```

```python
import math

import jax
import jax.numpy as jnp
import numpy as np
from jax import lax
from jax.experimental import pallas as pl
from jax.experimental.pallas import tpu as pltpu
from jax.sharding import PartitionSpec as P

F32, BF16 = jnp.float32, jnp.bfloat16
NX, NY, NZ, YR, ZC = 512, 128, 512, 2, 128
PART, MIG = 8192, 256
ROWS, COLS = 64, 4
XB = NX // ROWS
CHUNK = 1024
CELLS = YR * NX
STEP, COUPLING, STRETCH = 0.2, 0.5, 1.5


def periodic_compact(n):
    eye = np.eye(n)
    up, up2 = np.roll(eye, 1, 1), np.roll(eye, 2, 1)
    lhs = eye + (up + up.T) / 3.0
    rhs = (up - up.T) * 7.0 / 9.0 + (up2 - up2.T) / 36.0
    return np.linalg.solve(lhs, rhs)


def wall_compact(n):
    lhs, rhs = np.eye(n), np.zeros((n, n))
    for j in range(1, n - 1):
        near = j in (1, n - 2)
        lhs[j, j - 1] = lhs[j, j + 1] = 0.25 if near else 1.0 / 3.0
        rhs[j, j + 1] = 0.75 if near else 7.0 / 9.0
        rhs[j, j - 1] = -rhs[j, j + 1]
        if not near:
            rhs[j, j + 2], rhs[j, j - 2] = 1.0 / 36.0, -1.0 / 36.0
    lhs[0, 1] = lhs[n - 1, n - 2] = 2.0
    rhs[0, :3] = (-2.5, 2.0, 0.5)
    rhs[n - 1, n - 3 :] = (-0.5, -2.0, 2.5)
    eta = -1.0 + 2.0 * np.arange(n) / (n - 1)
    slope = STRETCH * (1.0 - np.tanh(STRETCH * eta) ** 2) / math.tanh(STRETCH)
    return np.linalg.solve(lhs, rhs) / slope[:, None]


def spectral(n):
    offset = np.arange(n)[:, None] - np.arange(n)[None, :]
    safe = np.where(offset == 0, 1, offset)
    value = math.pi / n * (1.0 - 2.0 * (offset % 2)) / np.tan(math.pi * safe / n)
    return np.where(offset == 0, 0.0, value)


def split_np(matrix):
    high = matrix.astype(np.float32).astype(BF16)
    low = (matrix - high.astype(np.float64)).astype(np.float32).astype(BF16)
    return high, low


def split(value):
    high = value.astype(BF16)
    return high, (value - high.astype(F32)).astype(BF16)


def constants():
    dx, dy, dz = periodic_compact(NX), wall_compact(NY), spectral(NZ)
    x_row = np.concatenate([dx[:128], (dx @ dx)[:128]], 0)
    z_t = np.concatenate([dz.T[:128], (dz @ dz).T[:128]], 0)
    x_high, x_low = split_np(x_row)
    z_high, z_low = split_np(z_t)
    y_high, y_low = split_np(np.concatenate([dy, dy @ dy], 0))
    y_three = np.concatenate([y_high, y_high, y_low], 1)
    return np.stack([x_high, x_low]), y_three, np.stack([z_high, z_low])


def nt(a, b):
    return lax.dot_general(a, b, (((1,), (1,)), ((), ())), preferred_element_type=F32)


def mm(a, b):
    return jnp.dot(a, b, preferred_element_type=F32)


def particle_kernel(counts, fields, records, response, cell, dest, slot, kept, deposit, outgoing, table, spilled):
    step = pl.program_id(0)

    @pl.when(step == 0)
    def _():
        for a in range(3):
            high, low = split(fields[a].reshape(CELLS, ZC).T)
            table[pl.ds(a * ZC, ZC), :] = high
            table[pl.ds((3 + a) * ZC, ZC), :] = low
        deposit[...] = jnp.zeros_like(deposit)
        spilled[...] = jnp.zeros_like(spilled)

    index = cell[...]
    row, lane = index // ZC, index % ZC
    local = step * CHUNK + lax.broadcasted_iota(jnp.int32, (1, CHUNK), 1)
    live = local < counts[0]
    in_row = lax.broadcasted_iota(jnp.int32, (CELLS, CHUNK), 0) == row
    hot = jnp.where(in_row, 1.0, 0.0).astype(BF16)
    in_lane = lax.broadcasted_iota(jnp.int32, (ZC, CHUNK), 0) == lane
    picked = mm(table[...], hot)
    fluid = []
    for a in range(3):
        both = picked[a * ZC : (a + 1) * ZC] + picked[(3 + a) * ZC : (4 + a) * ZC]
        fluid.append(jnp.sum(jnp.where(in_lane, both, 0.0), axis=0, keepdims=True))
    fluid = jnp.concatenate(fluid, axis=0)
    speed = records[3:6, :]
    drag = (fluid - speed) / response[...]
    velocity = speed + STEP * drag
    moved = jnp.concatenate([records[0:3, :] + STEP * velocity, velocity], axis=0)
    kept[...] = jnp.where(live & (dest[...] == 0), moved, 0.0)
    force = jnp.where(live, -COUPLING * drag, 0.0)
    spread = jnp.concatenate([jnp.where(in_lane, force[a : a + 1], 0.0) for a in range(3)], axis=0)
    high, low = split(spread)
    laid = nt(hot, high) + nt(hot, low)
    for a in range(3):
        deposit[a] += laid[:, a * ZC : (a + 1) * ZC]
    leaving = live & (dest[...] > 0)
    place = jnp.where(leaving, (dest[...] - 1) * 2 + slot[...] // 128, 8)
    in_half = lax.broadcasted_iota(jnp.int32, (8, CHUNK), 0) == place
    in_slot = lax.broadcasted_iota(jnp.int32, (128, CHUNK), 0) == slot[...] % 128
    slot_hot = jnp.where(in_slot, 1.0, 0.0).astype(BF16)
    parts = jnp.concatenate([jnp.where(in_half, moved[m : m + 1], 0.0) for m in range(6)], axis=0)
    high, low = split(parts)
    rest = (parts - high.astype(F32) - low.astype(F32)).astype(BF16)
    spilled[...] += nt(high, slot_hot) + nt(low, slot_hot) + nt(rest, slot_hot)

    @pl.when(step == pl.num_programs(0) - 1)
    def _():
        outgoing[...] = spilled[...]


def particles(fields, records, response, cell, counts, dest, slot):
    line = pl.BlockSpec((1, CHUNK), lambda s: (0, s))
    six = pl.BlockSpec((6, CHUNK), lambda s: (0, s))
    whole = pl.BlockSpec((4, YR, NX, ZC), lambda s: (0, 0, 0, 0), pipeline_mode=pl.Buffered(1))
    return pl.pallas_call(
        particle_kernel,
        grid=(PART // CHUNK,),
        in_specs=[pl.BlockSpec(memory_space=pltpu.SMEM), whole, six, line, line, line, line],
        out_specs=[
            six,
            pl.BlockSpec((3, CELLS, ZC), lambda s: (0, 0, 0)),
            pl.BlockSpec((48, 128), lambda s: (0, 0)),
        ],
        out_shape=[
            jax.ShapeDtypeStruct((6, PART), F32),
            jax.ShapeDtypeStruct((3, CELLS, ZC), F32),
            jax.ShapeDtypeStruct((48, 128), F32),
        ],
        scratch_shapes=[pltpu.VMEM((6 * ZC, CELLS), BF16), pltpu.VMEM((48, 128), F32)],
        compiler_params=pltpu.CompilerParams(vmem_limit_bytes=56 << 20),
        cost_estimate=pl.CostEstimate(flops=26_000_000_000, bytes_accessed=5_000_000, transcendentals=0),
        name="particles",
    )(counts, fields, records, response[None], cell[None], dest[None], slot[None])


def x_kernel(viscous, base, fields, speed, deposit, out, matrix):
    c = pl.program_id(0)

    @pl.when(c == 0)
    def _():
        for kind in range(2):
            for i in range(4):
                rows = pl.ds((kind * 4 + i) * 128, 128)
                for j in range(4):
                    block = (slice(kind * 128, (kind + 1) * 128), slice(((j - i) % 4) * 128, ((j - i) % 4 + 1) * 128))
                    high, low = base[(0,) + block], base[(1,) + block]
                    matrix[rows, pl.ds(j * 128, 128)] = high
                    matrix[rows, pl.ds(NX + j * 128, 128)] = high
                    matrix[rows, pl.ds(2 * NX + j * 128, 128)] = low

    value = jnp.concatenate([fields[0, y] for y in range(YR)], axis=1)
    high, low = split(value)
    result = mm(matrix[...], jnp.concatenate([high, low, high], axis=0))
    for y in range(YR):
        along, curve = result[:NX, y * ZC : (y + 1) * ZC], result[NX:, y * ZC : (y + 1) * ZC]
        add = jnp.where(c < 3, deposit[0, pl.ds(y * NX, NX), :], 0.0)
        out[0, y] = viscous[c] * curve - speed[0, y] * along + add


def x_terms(viscous, base, fields, deposit):
    block = (1, YR, NX, ZC)
    return pl.pallas_call(
        x_kernel,
        grid=(4,),
        in_specs=[
            pl.BlockSpec(memory_space=pltpu.SMEM),
            pl.BlockSpec((2, 256, NX), lambda c: (0, 0, 0)),
            pl.BlockSpec(block, lambda c: (c, 0, 0, 0)),
            pl.BlockSpec(block, lambda c: (0, 0, 0, 0)),
            pl.BlockSpec((1, CELLS, ZC), lambda c: (jnp.minimum(c, 2), 0, 0)),
        ],
        out_specs=pl.BlockSpec(block, lambda c: (c, 0, 0, 0)),
        out_shape=jax.ShapeDtypeStruct((4, YR, NX, ZC), F32),
        scratch_shapes=[pltpu.VMEM((2 * NX, 3 * NX), BF16)],
        compiler_params=pltpu.CompilerParams(vmem_limit_bytes=48 << 20),
        cost_estimate=pl.CostEstimate(flops=3_300_000_000, bytes_accessed=8_000_000, transcendentals=0),
        name="x_terms",
    )(viscous, base, fields, fields, deposit)


def y_kernel(viscous, matrix, value, speed, out):
    c = pl.program_id(0)
    wide = jnp.concatenate([value[:, 0, x, :] for x in range(XB)], axis=1)
    high, low = split(wide)
    result = mm(matrix[...], jnp.concatenate([high, low, high], axis=0))
    for x in range(XB):
        along, curve = result[:NY, x * ZC : (x + 1) * ZC], result[NY:, x * ZC : (x + 1) * ZC]
        out[:, 0, x, :] = viscous[c] * curve - speed[:, 0, x, :] * along


def y_terms(viscous, matrix, value):
    block = (NY, 1, XB, ZC)
    return pl.pallas_call(
        y_kernel,
        grid=(4,),
        in_specs=[
            pl.BlockSpec(memory_space=pltpu.SMEM),
            pl.BlockSpec((2 * NY, 3 * NY), lambda c: (0, 0)),
            pl.BlockSpec(block, lambda c: (0, c, 0, 0)),
            pl.BlockSpec(block, lambda c: (0, 1, 0, 0)),
        ],
        out_specs=pl.BlockSpec(block, lambda c: (0, c, 0, 0)),
        out_shape=jax.ShapeDtypeStruct((NY, 4, XB, ZC), F32),
        compiler_params=pltpu.CompilerParams(vmem_limit_bytes=32 << 20),
        cost_estimate=pl.CostEstimate(flops=800_000_000, bytes_accessed=5_000_000, transcendentals=0),
        name="y_terms",
    )(viscous, matrix, value, value)


def z_kernel(viscous, base, value, speed, out, matrix):
    c = pl.program_id(0)

    @pl.when(c == 0)
    def _():
        for kind in range(2):
            for i in range(4):
                rows = i * 128
                for j in range(4):
                    columns = pl.ds((kind * 4 + j) * 128, 128)
                    block = (slice(kind * 128, (kind + 1) * 128), slice(((j - i) % 4) * 128, ((j - i) % 4 + 1) * 128))
                    high, low = base[(0,) + block], base[(1,) + block]
                    matrix[pl.ds(rows, 128), columns] = high
                    matrix[pl.ds(NZ + rows, 128), columns] = high
                    matrix[pl.ds(2 * NZ + rows, 128), columns] = low

    wide = jnp.concatenate([value[p, 0].reshape(YR * 128, ZC) for p in range(COLS)], axis=1)
    high, low = split(wide)
    result = mm(jnp.concatenate([high, low, high], axis=1), matrix[...])
    for q in range(COLS):
        along, curve = result[:, q * ZC : (q + 1) * ZC], result[:, NZ + q * ZC : NZ + (q + 1) * ZC]
        speed_q = speed[q, 0].reshape(YR * 128, ZC)
        out[q, 0] = (viscous[c] * curve - speed_q * along).reshape(YR, 128, ZC)


def z_terms(viscous, base, value):
    block = (COLS, 1, YR, 128, ZC)
    return pl.pallas_call(
        z_kernel,
        grid=(4,),
        in_specs=[
            pl.BlockSpec(memory_space=pltpu.SMEM),
            pl.BlockSpec((2, 256, NZ), lambda c: (0, 0, 0)),
            pl.BlockSpec(block, lambda c: (0, c, 0, 0, 0)),
            pl.BlockSpec(block, lambda c: (0, 2, 0, 0, 0)),
        ],
        out_specs=pl.BlockSpec(block, lambda c: (0, c, 0, 0, 0)),
        out_shape=jax.ShapeDtypeStruct((COLS, 4, YR, 128, ZC), F32),
        scratch_shapes=[pltpu.VMEM((3 * NZ, 2 * NZ), BF16)],
        compiler_params=pltpu.CompilerParams(vmem_limit_bytes=48 << 20),
        cost_estimate=pl.CostEstimate(flops=3_300_000_000, bytes_accessed=6_000_000, transcendentals=0),
        name="z_terms",
    )(viscous, base, value, value)


def sum_kernel(x_part, y_part, z_part, out):
    for y in range(YR):
        for q in range(COLS):
            rows = pl.ds(q * 128, 128)
            from_y = y_part[pl.ds(q * 16, 16), y, 0].reshape(128, ZC)
            out[0, y, rows, :] = x_part[0, y, rows, :] + from_y + z_part[q, 0, y]


def total(x_part, y_part, z_part):
    block = (1, YR, NX, ZC)
    return pl.pallas_call(
        sum_kernel,
        grid=(4,),
        in_specs=[
            pl.BlockSpec(block, lambda c: (c, 0, 0, 0)),
            pl.BlockSpec((ROWS, YR, 1, XB, ZC), lambda c: (0, 0, c, 0, 0)),
            pl.BlockSpec((COLS, 1, YR, 128, ZC), lambda c: (0, c, 0, 0, 0)),
        ],
        out_specs=pl.BlockSpec(block, lambda c: (c, 0, 0, 0)),
        out_shape=jax.ShapeDtypeStruct((4, YR, NX, ZC), F32),
        compiler_params=pltpu.CompilerParams(vmem_limit_bytes=32 << 20),
        cost_estimate=pl.CostEstimate(flops=2_000_000, bytes_accessed=8_000_000, transcendentals=0),
        name="total",
    )(x_part, y_part, z_part)


def swap(block, axis):
    return lax.all_to_all(block, axis, split_axis=0, concat_axis=0, tiled=True)


def on_device(fields, diffusivity, records, response_time, cell_index, counts, destination, slot):
    x_base, y_matrix, z_base = (jnp.asarray(m) for m in constants())
    to_y = fields.reshape(4, YR, ROWS, XB, ZC).transpose(2, 1, 0, 3, 4)
    to_z = fields.reshape(4, YR, COLS, 128, ZC).transpose(2, 0, 1, 3, 4)
    at_z = swap(to_z, "col")
    at_y = swap(to_y, "row")
    kept, deposit, outgoing = particles(
        fields, records, response_time, cell_index, counts, destination, slot
    )
    x_part = x_terms(diffusivity, x_base, fields, deposit)
    y_out = y_terms(diffusivity, y_matrix, at_y.reshape(NY, 4, XB, ZC))
    y_part = swap(y_out.reshape(ROWS, YR, 4, XB, ZC), "row")
    z_part = swap(z_terms(diffusivity, z_base, at_z), "col")
    tendency = total(x_part, y_part, z_part)
    outgoing = outgoing.reshape(6, 4, MIG)
    received = []
    for direction, step in ((0, 1), (1, -1)):
        pairs = [(r, r + step) for r in range(ROWS) if 0 <= r + step < ROWS]
        received.append(lax.ppermute(outgoing[:, direction], "row", pairs))
    for direction, step in ((2, 1), (3, -1)):
        pairs = [(c, (c + step) % COLS) for c in range(COLS)]
        received.append(lax.ppermute(outgoing[:, direction], "col", pairs))
    return tendency, kept, jnp.stack(received, axis=0)


def solution(mesh):
    both = ("row", "col")
    return jax.shard_map(
        on_device,
        mesh=mesh,
        in_specs=(
            P(None, "row", None, "col"),
            P(),
            P(None, both),
            P(both),
            P(both),
            P(both),
            P(both),
            P(both),
        ),
        out_specs=(P(None, "row", None, "col"), P(None, both), P(None, None, both)),
        check_vma=False,
    )
```

```python
import math

import jax
import jax.numpy as jnp
import numpy as np
from jax import lax
from jax.experimental import pallas as pl
from jax.experimental.pallas import tpu as pltpu
from jax.sharding import PartitionSpec as P

F32, BF16 = jnp.float32, jnp.bfloat16
NX, NY, NZ, YR, ZC = 512, 128, 512, 2, 128
PART, MIG = 8192, 256
ROWS, COLS = 64, 4
XB = NX // ROWS
CHUNK = 1024
MESH = pl.DeviceIdType.MESH
CELLS = YR * NX
STEP, COUPLING, STRETCH = 0.2, 0.5, 1.5


def periodic_compact(n):
    eye = np.eye(n)
    up, up2 = np.roll(eye, 1, 1), np.roll(eye, 2, 1)
    lhs = eye + (up + up.T) / 3.0
    rhs = (up - up.T) * 7.0 / 9.0 + (up2 - up2.T) / 36.0
    return np.linalg.solve(lhs, rhs)


def wall_compact(n):
    lhs, rhs = np.eye(n), np.zeros((n, n))
    for j in range(1, n - 1):
        near = j in (1, n - 2)
        lhs[j, j - 1] = lhs[j, j + 1] = 0.25 if near else 1.0 / 3.0
        rhs[j, j + 1] = 0.75 if near else 7.0 / 9.0
        rhs[j, j - 1] = -rhs[j, j + 1]
        if not near:
            rhs[j, j + 2], rhs[j, j - 2] = 1.0 / 36.0, -1.0 / 36.0
    lhs[0, 1] = lhs[n - 1, n - 2] = 2.0
    rhs[0, :3] = (-2.5, 2.0, 0.5)
    rhs[n - 1, n - 3 :] = (-0.5, -2.0, 2.5)
    eta = -1.0 + 2.0 * np.arange(n) / (n - 1)
    slope = STRETCH * (1.0 - np.tanh(STRETCH * eta) ** 2) / math.tanh(STRETCH)
    return np.linalg.solve(lhs, rhs) / slope[:, None]


def spectral(n):
    offset = np.arange(n)[:, None] - np.arange(n)[None, :]
    safe = np.where(offset == 0, 1, offset)
    value = math.pi / n * (1.0 - 2.0 * (offset % 2)) / np.tan(math.pi * safe / n)
    return np.where(offset == 0, 0.0, value)


def split_np(matrix):
    high = matrix.astype(np.float32).astype(BF16)
    low = (matrix - high.astype(np.float64)).astype(np.float32).astype(BF16)
    return high, low


def split(value):
    high = value.astype(BF16)
    return high, (value - high.astype(F32)).astype(BF16)


def constants():
    dx, dy, dz = periodic_compact(NX), wall_compact(NY), spectral(NZ)
    x_row = np.concatenate([dx[:128], (dx @ dx)[:128]], 0)
    z_t = np.concatenate([dz.T[:128], (dz @ dz).T[:128]], 0)
    x_high, x_low = split_np(x_row)
    z_high, z_low = split_np(z_t)
    y_high, y_low = split_np(np.concatenate([dy, dy @ dy], 0))
    y_three = np.concatenate([y_high, y_high, y_low], 1)
    return np.stack([x_high, x_low]), y_three, np.stack([z_high, z_low])


def nt(a, b):
    return lax.dot_general(a, b, (((1,), (1,)), ((), ())), preferred_element_type=F32)


def mm(a, b):
    return jnp.dot(a, b, preferred_element_type=F32)


def expand(base, matrix, size, by_rows):
    for kind in range(2):
        for i in range(4):
            for j in range(4):
                at = ((j - i) if by_rows else (i + j)) % 4
                block = (slice(kind * 128, (kind + 1) * 128), slice(at * 128, (at + 1) * 128))
                for place, part in enumerate((0, 0, 1)):
                    tile = base[(part,) + block]
                    if by_rows:
                        matrix[pl.ds((kind * 4 + i) * 128, 128), pl.ds(place * size + j * 128, 128)] = tile
                    else:
                        matrix[pl.ds(place * size + i * 128, 128), pl.ds((kind * 4 + j) * 128, 128)] = tile


def step_kernel(
    counts, viscous, x_base, y_matrix, z_base, fields, records, response, cell, dest, slot,
    tendency, kept, arrivals,
    at_y, at_z, y_out, z_out, back_y, back_z, x_matrix, z_matrix, table, deposit, spilled, packed, landed,
    y_send, y_recv, back_y_send, back_y_recv, z_send, z_recv, back_z_send, back_z_recv, move_send, move_recv,
):
    r, c = lax.axis_index("row"), lax.axis_index("col")
    x_here = pl.ds(pl.multiple_of(c * 128, 128), 128)

    barrier = pltpu.get_barrier_semaphore()

    def greet(i, _):
        pl.semaphore_signal(barrier, inc=1, device_id=(lax.rem(r + i, ROWS), c), device_id_type=MESH)
        return 0

    lax.fori_loop(1, ROWS, greet, 0)
    for d in range(1, COLS):
        pl.semaphore_signal(barrier, inc=1, device_id=(r, lax.rem(c + d, COLS)), device_id_type=MESH)
    pl.semaphore_wait(barrier, ROWS + COLS - 2)

    def peer(i):
        half = lax.div(i + 1, 2)
        return lax.rem(r + jnp.where(lax.rem(i, 2) == 1, half, ROWS - half), ROWS)

    def to_y(p, from_row):
        return pltpu.make_async_remote_copy(
            src_ref=fields.at[:, :, pl.ds(pl.multiple_of(p * XB, XB), XB), :],
            dst_ref=at_y.at[:, pl.ds(from_row * YR, YR)],
            send_sem=y_send.at[p],
            recv_sem=y_recv.at[from_row],
            device_id=(p, c),
            device_id_type=MESH,
        )

    def from_y(p, from_row):
        return pltpu.make_async_remote_copy(
            src_ref=y_out.at[:, pl.ds(p * YR, YR)],
            dst_ref=back_y.at[:, :, pl.ds(pl.multiple_of(from_row * XB, XB), XB), :],
            send_sem=back_y_send.at[p],
            recv_sem=back_y_recv.at[from_row],
            device_id=(p, c),
            device_id_type=MESH,
        )

    def to_z(d, q):
        to = lax.rem(c + d, COLS)
        return pltpu.make_async_remote_copy(
            src_ref=fields.at[q, :, pl.ds(pl.multiple_of(to * 128, 128), 128), :],
            dst_ref=at_z.at[d - 1, q],
            send_sem=z_send.at[d, q],
            recv_sem=z_recv.at[d, q],
            device_id=(r, to),
            device_id_type=MESH,
        )

    def from_z(d, q, sender):
        return pltpu.make_async_remote_copy(
            src_ref=z_out.at[d, q],
            dst_ref=back_z.at[q, :, pl.ds(pl.multiple_of(sender * 128, 128), 128), :],
            send_sem=back_z_send.at[d, q],
            recv_sem=back_z_recv.at[d, q],
            device_id=(r, lax.rem(c + d, COLS)),
            device_id_type=MESH,
        )

    def start_z(q, _):
        for d in (1, 3, 2):
            to_z(d, q).start()
        return 0

    def start_y(i, _):
        to_y(peer(i), r).start()
        return 0

    lax.fori_loop(0, 4, start_z, 0)
    lax.fori_loop(1, ROWS, start_y, 0)
    at_y[:, pl.ds(r * YR, YR)] = fields[:, :, pl.ds(pl.multiple_of(r * XB, XB), XB), :]

    for a in range(3):
        high, low = split(fields[a].reshape(CELLS, ZC).T)
        table[pl.ds(a * ZC, ZC), :] = high
        table[pl.ds((3 + a) * ZC, ZC), :] = low
    deposit[...] = jnp.zeros_like(deposit)
    spilled[...] = jnp.zeros_like(spilled)
    expand(x_base, x_matrix, NX, True)
    expand(z_base, z_matrix, NZ, False)

    def particles(step, _):
        here = pl.ds(pl.multiple_of(step * CHUNK, CHUNK), CHUNK)
        index = cell[:, here]
        row, lane = index // ZC, index % ZC
        local = step * CHUNK + lax.broadcasted_iota(jnp.int32, (1, CHUNK), 1)
        live = local < counts[0]
        in_row = lax.broadcasted_iota(jnp.int32, (CELLS, CHUNK), 0) == row
        hot = jnp.where(in_row, 1.0, 0.0).astype(BF16)
        in_lane = lax.broadcasted_iota(jnp.int32, (ZC, CHUNK), 0) == lane
        picked = mm(table[...], hot)
        fluid = []
        for a in range(3):
            both = picked[a * ZC : (a + 1) * ZC] + picked[(3 + a) * ZC : (4 + a) * ZC]
            fluid.append(jnp.sum(jnp.where(in_lane, both, 0.0), axis=0, keepdims=True))
        fluid = jnp.concatenate(fluid, axis=0)
        speed = records[3:6, here]
        drag = (fluid - speed) / response[:, here]
        velocity = speed + STEP * drag
        moved = jnp.concatenate([records[0:3, here] + STEP * velocity, velocity], axis=0)
        to = dest[:, here]
        kept[:, here] = jnp.where(live & (to == 0), moved, 0.0)
        force = jnp.where(live, -COUPLING * drag, 0.0)
        spread = jnp.concatenate([jnp.where(in_lane, force[a : a + 1], 0.0) for a in range(3)], axis=0)
        high, low = split(spread)
        laid = nt(hot, high) + nt(hot, low)
        for a in range(3):
            deposit[a] += laid[:, a * ZC : (a + 1) * ZC]
        spot = slot[:, here]
        place = jnp.where(live & (to > 0), (to - 1) * 2 + spot // 128, 8)
        in_slot = lax.broadcasted_iota(jnp.int32, (128, CHUNK), 0) == spot % 128
        slot_hot = jnp.where(in_slot, 1.0, 0.0).astype(BF16)
        eight = jnp.concatenate([moved, jnp.zeros((2, CHUNK), F32)], axis=0)
        parts = jnp.concatenate([jnp.where(place == h, eight, 0.0) for h in range(8)], axis=0)
        high, low = split(parts)
        rest = (parts - high.astype(F32) - low.astype(F32)).astype(BF16)
        spilled[...] += nt(high, slot_hot) + nt(low, slot_hot) + nt(rest, slot_hot)
        return 0

    lax.fori_loop(0, PART // CHUNK, particles, 0)
    for d in range(4):
        for h in range(2):
            packed[d, :, pl.ds(h * 128, 128)] = spilled[pl.ds((2 * d + h) * 8, 8), :]

    def x_terms(q, _):
        value = jnp.concatenate([fields[q, y] for y in range(YR)], axis=1)
        high, low = split(value)
        result = mm(x_matrix[...], jnp.concatenate([high, low, high], axis=0))
        for y in range(YR):
            along, curve = result[:NX, y * ZC : (y + 1) * ZC], result[NX:, y * ZC : (y + 1) * ZC]
            tendency[q, y] = viscous[q] * curve - fields[0, y] * along
        return 0

    lax.fori_loop(0, 4, x_terms, 0)
    for a in range(3):
        for y in range(YR):
            tendency[a, y] += deposit[a, pl.ds(y * NX, NX), :]

    def move(d):
        target = ((lax.rem(r + 1, ROWS), c), (lax.rem(r + ROWS - 1, ROWS), c), (r, lax.rem(c + 1, COLS)), (r, lax.rem(c + 3, COLS)))[d]
        return pltpu.make_async_remote_copy(
            src_ref=packed.at[d],
            dst_ref=landed.at[d],
            send_sem=move_send.at[d],
            recv_sem=move_recv.at[d],
            device_id=target,
            device_id_type=MESH,
        )

    @pl.when(r < ROWS - 1)
    def _():
        move(0).start()

    @pl.when(r > 0)
    def _():
        move(1).start()

    move(2).start()
    move(3).start()

    def wait_y(i, _):
        p = lax.rem(r + i, ROWS)
        to_y(p, p).wait_recv()
        return 0

    lax.fori_loop(1, ROWS, wait_y, 0)

    def y_terms(q, _):
        wide = jnp.concatenate([at_y[q, :, x, :] for x in range(XB)], axis=1)
        high, low = split(wide)
        result = mm(y_matrix[...], jnp.concatenate([high, low, high], axis=0))
        for x in range(XB):
            along, curve = result[:NY, x * ZC : (x + 1) * ZC], result[NY:, x * ZC : (x + 1) * ZC]
            y_out[q, :, x, :] = viscous[q] * curve - at_y[1, :, x, :] * along
        return 0

    lax.fori_loop(0, 4, y_terms, 0)
    back_y[:, :, pl.ds(pl.multiple_of(r * XB, XB), XB), :] = y_out[:, pl.ds(r * YR, YR)]

    def start_back_y(i, _):
        from_y(peer(i), r).start()
        return 0

    lax.fori_loop(1, ROWS, start_back_y, 0)

    def z_block(q, d):
        block = fields[q, :, x_here, :] if d == 0 else at_z[d - 1, q]
        return block.reshape(YR * 128, ZC)

    for d in range(1, COLS):
        to_z(d, 2).wait_recv()

    def z_terms(q, _):
        @pl.when(q != 2)
        def _():
            for d in range(1, COLS):
                to_z(d, q).wait_recv()

        wide = jnp.concatenate([z_block(q, d) for d in range(COLS)], axis=1)
        high, low = split(wide)
        result = mm(jnp.concatenate([high, low, high], axis=1), z_matrix[...])
        for e in range(COLS):
            along, curve = result[:, e * ZC : (e + 1) * ZC], result[:, NZ + e * ZC : NZ + (e + 1) * ZC]
            term = viscous[q] * curve - z_block(2, (COLS - e) % COLS) * along
            z_out[e, q] = term.reshape(YR, 128, ZC)
        for d in (1, 3, 2):
            from_z(d, q, c).start()
        return 0

    lax.fori_loop(0, 4, z_terms, 0)
    for q in range(4):
        tendency[q, :, x_here, :] += z_out[0, q]

    def wait_back_y(i, _):
        p = lax.rem(r + i, ROWS)
        from_y(p, p).wait_recv()
        return 0

    lax.fori_loop(1, ROWS, wait_back_y, 0)

    def finish(q, _):
        tendency[q] += back_y[q]
        for d in range(1, COLS):
            sender = lax.rem(c + COLS - d, COLS)
            from_z(d, q, sender).wait_recv()
            rows = pl.ds(pl.multiple_of(sender * 128, 128), 128)
            tendency[q, :, rows, :] += back_z[q, :, rows, :]
        return 0

    lax.fori_loop(0, 4, finish, 0)

    @pl.when(r > 0)
    def _():
        move(0).wait_recv()
        arrivals[0] = landed[0, 0:6, :]

    @pl.when(r == 0)
    def _():
        arrivals[0] = jnp.zeros((6, MIG), F32)

    @pl.when(r < ROWS - 1)
    def _():
        move(1).wait_recv()
        arrivals[1] = landed[1, 0:6, :]

    @pl.when(r == ROWS - 1)
    def _():
        arrivals[1] = jnp.zeros((6, MIG), F32)

    for d in (2, 3):
        move(d).wait_recv()
        arrivals[d] = landed[d, 0:6, :]

    @pl.when(r < ROWS - 1)
    def _():
        move(0).wait_send()

    @pl.when(r > 0)
    def _():
        move(1).wait_send()

    move(2).wait_send()
    move(3).wait_send()

    def sent_y(i, _):
        p = lax.rem(r + i, ROWS)
        to_y(p, p).wait_send()
        from_y(p, p).wait_send()
        return 0

    lax.fori_loop(1, ROWS, sent_y, 0)

    def sent_z(q, _):
        for d in range(1, COLS):
            to_z(d, q).wait_send()
            from_z(d, q, c).wait_send()
        return 0

    lax.fori_loop(0, 4, sent_z, 0)


def on_device(fields, diffusivity, records, response_time, cell_index, counts, destination, slot):
    x_base, y_matrix, z_base = (jnp.asarray(m) for m in constants())
    vmem, smem = pl.BlockSpec(memory_space=pltpu.VMEM), pl.BlockSpec(memory_space=pltpu.SMEM)
    dma = pltpu.SemaphoreType.DMA
    return pl.pallas_call(
        step_kernel,
        in_specs=[smem, smem] + [vmem] * 9,
        out_specs=[vmem] * 3,
        out_shape=[
            jax.ShapeDtypeStruct((4, YR, NX, ZC), F32),
            jax.ShapeDtypeStruct((6, PART), F32),
            jax.ShapeDtypeStruct((4, 6, MIG), F32),
        ],
        scratch_shapes=[
            pltpu.VMEM((4, NY, XB, ZC), F32),
            pltpu.VMEM((COLS - 1, 4, YR, 128, ZC), F32),
            pltpu.VMEM((4, NY, XB, ZC), F32),
            pltpu.VMEM((COLS, 4, YR, 128, ZC), F32),
            pltpu.VMEM((4, YR, NX, ZC), F32),
            pltpu.VMEM((4, YR, NX, ZC), F32),
            pltpu.VMEM((2 * NX, 3 * NX), BF16),
            pltpu.VMEM((3 * NZ, 2 * NZ), BF16),
            pltpu.VMEM((6 * ZC, CELLS), BF16),
            pltpu.VMEM((3, CELLS, ZC), F32),
            pltpu.VMEM((64, 128), F32),
            pltpu.VMEM((4, 8, MIG), F32),
            pltpu.VMEM((4, 8, MIG), F32),
            dma((ROWS,)), dma((ROWS,)), dma((ROWS,)), dma((ROWS,)),
            dma((COLS, 4)), dma((COLS, 4)), dma((COLS, 4)), dma((COLS, 4)),
            dma((4,)), dma((4,)),
        ],
        compiler_params=pltpu.CompilerParams(
            collective_id=0, has_side_effects=True, vmem_limit_bytes=60 << 20
        ),
        name="whole_step",
    )(
        counts, diffusivity, x_base, y_matrix, z_base, fields, records,
        response_time[None], cell_index[None], destination[None], slot[None],
    )


def solution(mesh):
    both = ("row", "col")
    return jax.shard_map(
        on_device,
        mesh=mesh,
        in_specs=(
            P(None, "row", None, "col"),
            P(),
            P(None, both),
            P(both),
            P(both),
            P(both),
            P(both),
            P(both),
        ),
        out_specs=(P(None, "row", None, "col"), P(None, both), P(None, None, both)),
        check_vma=False,
    )
```

```python
import math

import jax
import jax.numpy as jnp
import numpy as np
from jax import lax
from jax.experimental import pallas as pl
from jax.experimental.pallas import tpu as pltpu
from jax.sharding import PartitionSpec as P

F32, BF16 = jnp.float32, jnp.bfloat16
NX, NY, NZ, YR, ZC = 512, 128, 512, 2, 128
PART, MIG = 8192, 256
ROWS, COLS = 64, 4
HALF = ROWS // 2
XB = NX // HALF
YH = NY // 2
RANK, PAD = 28, 32
CHUNK = 1024
EARLY = 5
VLIM = 46
MESH = pl.DeviceIdType.MESH
CELLS = YR * NX
STEP, COUPLING, STRETCH = 0.2, 0.5, 1.5


def periodic_compact(n):
    eye = np.eye(n)
    up, up2 = np.roll(eye, 1, 1), np.roll(eye, 2, 1)
    lhs = eye + (up + up.T) / 3.0
    rhs = (up - up.T) * 7.0 / 9.0 + (up2 - up2.T) / 36.0
    return np.linalg.solve(lhs, rhs)


def wall_compact(n):
    lhs, rhs = np.eye(n), np.zeros((n, n))
    for j in range(1, n - 1):
        near = j in (1, n - 2)
        lhs[j, j - 1] = lhs[j, j + 1] = 0.25 if near else 1.0 / 3.0
        rhs[j, j + 1] = 0.75 if near else 7.0 / 9.0
        rhs[j, j - 1] = -rhs[j, j + 1]
        if not near:
            rhs[j, j + 2], rhs[j, j - 2] = 1.0 / 36.0, -1.0 / 36.0
    lhs[0, 1] = lhs[n - 1, n - 2] = 2.0
    rhs[0, :3] = (-2.5, 2.0, 0.5)
    rhs[n - 1, n - 3 :] = (-0.5, -2.0, 2.5)
    eta = -1.0 + 2.0 * np.arange(n) / (n - 1)
    slope = STRETCH * (1.0 - np.tanh(STRETCH * eta) ** 2) / math.tanh(STRETCH)
    return np.linalg.solve(lhs, rhs) / slope[:, None]


def spectral(n):
    offset = np.arange(n)[:, None] - np.arange(n)[None, :]
    safe = np.where(offset == 0, 1, offset)
    value = math.pi / n * (1.0 - 2.0 * (offset % 2)) / np.tan(math.pi * safe / n)
    return np.where(offset == 0, 0.0, value)


def split_np(matrix):
    high = matrix.astype(np.float32).astype(BF16)
    low = (matrix - high.astype(np.float64)).astype(np.float32).astype(BF16)
    return high, low


def split(value):
    high = value.astype(BF16)
    return high, (value - high.astype(F32)).astype(BF16)


def constants():
    dx, dy, dz = periodic_compact(NX), wall_compact(NY), spectral(NZ)
    x_row = np.concatenate([dx[:128], (dx @ dx)[:128]], 0)
    z_t = np.concatenate([dz.T[:128], (dz @ dz).T[:128]], 0)
    x_high, x_low = split_np(x_row)
    z_high, z_low = split_np(z_t)
    halves = [np.concatenate([np.arange(b, b + 16) for b in range(16 * k, NY, 32)]) for k in range(2)]
    own, give = [], [None, None]
    for k, (mine, other) in enumerate((halves, halves[::-1])):
        both = np.concatenate([dy[mine], (dy @ dy)[mine]], 0)
        left, scale, right = np.linalg.svd(both[:, other])
        assert scale[RANK] < 1e-13 * scale[0]
        reached = np.zeros((2 * YH, PAD))
        reached[:, :RANK] = left[:, :RANK] * scale[:RANK]
        high, low = split_np(np.concatenate([both[:, mine], reached], 1))
        own.append(np.concatenate([high, high, low], 1))
        wanted = np.zeros((PAD, YH))
        wanted[:RANK] = right[:RANK]
        high, low = split_np(wanted)
        give[1 - k] = np.concatenate([high, high, low], 1)
    return np.stack([x_high, x_low]), np.stack(own), np.stack(give), np.stack([z_high, z_low])


def nt(a, b):
    return lax.dot_general(a, b, (((1,), (1,)), ((), ())), preferred_element_type=F32)


def mm(a, b):
    return jnp.dot(a, b, preferred_element_type=F32)


def expand(base, matrix, size, by_rows):
    for kind in range(2):
        for i in range(4):
            for j in range(4):
                at = ((j - i) if by_rows else (i + j)) % 4
                block = (slice(kind * 128, (kind + 1) * 128), slice(at * 128, (at + 1) * 128))
                for place, part in enumerate((0, 0, 1)):
                    tile = base[(part,) + block]
                    if by_rows:
                        matrix[pl.ds((kind * 4 + i) * 128, 128), pl.ds(place * size + j * 128, 128)] = tile
                    else:
                        matrix[pl.ds(place * size + i * 128, 128), pl.ds((kind * 4 + j) * 128, 128)] = tile


def step_kernel(
    counts, viscous, x_base, y_matrix, y_give, z_base, fields, records, response, cell, dest, slot,
    tendency, kept, arrivals,
    at_y, at_z, y_out, z_out, back_y, back_z, x_matrix, z_matrix, table, deposit, spilled, packed, landed, given, taken,
    y_send, y_recv, back_y_send, back_y_recv, z_send, z_recv, back_z_send, back_z_recv, move_send, move_recv, give_send, give_recv,
):
    r, c = lax.axis_index("row"), lax.axis_index("col")
    side = lax.rem(lax.div(r, 8), 2)
    h = lax.div(r, 16) * 8 + lax.rem(r, 8)
    partner = r + 8 - 16 * side

    def row_of(p):
        return lax.div(p, 8) * 16 + side * 8 + lax.rem(p, 8)

    x_here = pl.ds(pl.multiple_of(c * 128, 128), 128)

    barrier = pltpu.get_barrier_semaphore()

    def greet(i, _):
        target = (row_of(lax.rem(h + i, HALF)), c)
        pl.semaphore_signal(barrier, inc=1, device_id=target, device_id_type=MESH)
        return 0

    lax.fori_loop(1, HALF, greet, 0)
    for row in (partner, lax.rem(r + 1, ROWS), lax.rem(r + ROWS - 1, ROWS)):
        pl.semaphore_signal(barrier, inc=1, device_id=(row, c), device_id_type=MESH)
    for d in range(1, COLS):
        pl.semaphore_signal(barrier, inc=1, device_id=(r, lax.rem(c + d, COLS)), device_id_type=MESH)
    pl.semaphore_wait(barrier, HALF - 1 + 3 + COLS - 1)

    def peer(i):
        half = lax.div(i + 1, 2)
        return lax.rem(h + jnp.where(lax.rem(i, 2) == 1, half, HALF - half), HALF)

    def order(i):
        return jnp.where(i == 0, 2, jnp.where(i == 3, 3, i - 1))

    def give(q):
        return pltpu.make_async_remote_copy(
            src_ref=given.at[q, pl.ds(0, RANK)],
            dst_ref=taken.at[q, pl.ds(0, RANK)],
            send_sem=give_send.at[q],
            recv_sem=give_recv.at[q],
            device_id=(partner, c),
            device_id_type=MESH,
        )

    def to_y(p, from_row):
        return pltpu.make_async_remote_copy(
            src_ref=fields.at[:, :, pl.ds(pl.multiple_of(p * XB, XB), XB), :],
            dst_ref=at_y.at[:, pl.ds(from_row * YR, YR)],
            send_sem=y_send.at[p],
            recv_sem=y_recv.at[from_row],
            device_id=(row_of(p), c),
            device_id_type=MESH,
        )

    def from_y(p, from_row):
        return pltpu.make_async_remote_copy(
            src_ref=y_out.at[:, pl.ds(p * YR, YR)],
            dst_ref=back_y.at[:, :, pl.ds(pl.multiple_of(from_row * XB, XB), XB), :],
            send_sem=back_y_send.at[p],
            recv_sem=back_y_recv.at[from_row],
            device_id=(row_of(p), c),
            device_id_type=MESH,
        )

    def to_z(d, q):
        to = lax.rem(c + d, COLS)
        return pltpu.make_async_remote_copy(
            src_ref=fields.at[q, :, pl.ds(pl.multiple_of(to * 128, 128), 128), :],
            dst_ref=at_z.at[d - 1, q],
            send_sem=z_send.at[d, q],
            recv_sem=z_recv.at[d, q],
            device_id=(r, to),
            device_id_type=MESH,
        )

    def from_z(d, q, sender):
        return pltpu.make_async_remote_copy(
            src_ref=z_out.at[d, q],
            dst_ref=back_z.at[q, :, pl.ds(pl.multiple_of(sender * 128, 128), 128), :],
            send_sem=back_z_send.at[d, q],
            recv_sem=back_z_recv.at[d, q],
            device_id=(r, lax.rem(c + d, COLS)),
            device_id_type=MESH,
        )

    def start_z(i, _):
        for d in (1, 3, 2):
            to_z(d, order(i)).start()
        return 0

    def start_y(i, _):
        to_y(peer(i), h).start()
        return 0

    lax.fori_loop(0, 1, start_z, 0)
    lax.fori_loop(1, HALF, start_y, 0)
    lax.fori_loop(1, 3, start_z, 0)
    at_y[:, pl.ds(h * YR, YR)] = fields[:, :, pl.ds(pl.multiple_of(h * XB, XB), XB), :]
    taken[:, pl.ds(RANK, PAD - RANK)] = jnp.zeros((4, PAD - RANK, XB, ZC), F32)

    for a in range(3):
        high, low = split(fields[a].reshape(CELLS, ZC).T)
        table[pl.ds(a * ZC, ZC), :] = high
        table[pl.ds((3 + a) * ZC, ZC), :] = low
    deposit[...] = jnp.zeros_like(deposit)
    spilled[...] = jnp.zeros_like(spilled)
    expand(x_base, x_matrix, NX, True)
    expand(z_base, z_matrix, NZ, False)

    def particles(step, _):
        here = pl.ds(pl.multiple_of(step * CHUNK, CHUNK), CHUNK)
        index = cell[:, here]
        row, lane = index // ZC, index % ZC
        local = step * CHUNK + lax.broadcasted_iota(jnp.int32, (1, CHUNK), 1)
        live = local < counts[0]
        in_row = lax.broadcasted_iota(jnp.int32, (CELLS, CHUNK), 0) == row
        hot = jnp.where(in_row, 1.0, 0.0).astype(BF16)
        in_lane = lax.broadcasted_iota(jnp.int32, (ZC, CHUNK), 0) == lane
        picked = mm(table[...], hot)
        fluid = []
        for a in range(3):
            both = picked[a * ZC : (a + 1) * ZC] + picked[(3 + a) * ZC : (4 + a) * ZC]
            fluid.append(jnp.sum(jnp.where(in_lane, both, 0.0), axis=0, keepdims=True))
        fluid = jnp.concatenate(fluid, axis=0)
        speed = records[3:6, here]
        drag = (fluid - speed) / response[:, here]
        velocity = speed + STEP * drag
        moved = jnp.concatenate([records[0:3, here] + STEP * velocity, velocity], axis=0)
        to = dest[:, here]
        kept[:, here] = jnp.where(live & (to == 0), moved, 0.0)
        force = jnp.where(live, -COUPLING * drag, 0.0)
        spread = jnp.concatenate([jnp.where(in_lane, force[a : a + 1], 0.0) for a in range(3)], axis=0)
        high, low = split(spread)
        laid = nt(hot, high) + nt(hot, low)
        for a in range(3):
            deposit[a] += laid[:, a * ZC : (a + 1) * ZC]
        spot = slot[:, here]
        place = jnp.where(live & (to > 0), (to - 1) * 2 + spot // 128, 8)
        in_slot = lax.broadcasted_iota(jnp.int32, (128, CHUNK), 0) == spot % 128
        slot_hot = jnp.where(in_slot, 1.0, 0.0).astype(BF16)
        eight = jnp.concatenate([moved, jnp.zeros((2, CHUNK), F32)], axis=0)
        parts = jnp.concatenate([jnp.where(place == spot_at, eight, 0.0) for spot_at in range(8)], axis=0)
        high, low = split(parts)
        rest = (parts - high.astype(F32) - low.astype(F32)).astype(BF16)
        spilled[...] += nt(high, slot_hot) + nt(low, slot_hot) + nt(rest, slot_hot)
        return 0

    lax.fori_loop(0, EARLY, particles, 0)

    def wait_y(i, _):
        p = lax.rem(h + i, HALF)
        to_y(p, p).wait_recv()
        return 0

    lax.fori_loop(1, HALF, wait_y, 0)

    def wanted(q, _):
        wide = jnp.concatenate([at_y[q, :, x, :] for x in range(XB)], axis=1)
        high, low = split(wide)
        result = mm(y_give[side], jnp.concatenate([high, low, high], axis=0))
        for x in range(XB):
            given[q, :, x, :] = result[:, x * ZC : (x + 1) * ZC]
        return 0

    lax.fori_loop(0, 4, wanted, 0)
    for q in range(4):
        give(q).start()
    lax.fori_loop(3, 4, start_z, 0)

    lax.fori_loop(EARLY, PART // CHUNK, particles, 0)
    for d in range(4):
        for part in range(2):
            packed[d, :, pl.ds(part * 128, 128)] = spilled[pl.ds((2 * d + part) * 8, 8), :]

    def x_terms(q, _):
        value = jnp.concatenate([fields[q, y] for y in range(YR)], axis=1)
        high, low = split(value)
        result = mm(x_matrix[...], jnp.concatenate([high, low, high], axis=0))
        for y in range(YR):
            along, curve = result[:NX, y * ZC : (y + 1) * ZC], result[NX:, y * ZC : (y + 1) * ZC]
            tendency[q, y] = viscous[q] * curve - fields[0, y] * along
        return 0

    lax.fori_loop(0, 4, x_terms, 0)
    for a in range(3):
        for y in range(YR):
            tendency[a, y] += deposit[a, pl.ds(y * NX, NX), :]

    def move(d):
        target = ((lax.rem(r + 1, ROWS), c), (lax.rem(r + ROWS - 1, ROWS), c), (r, lax.rem(c + 1, COLS)), (r, lax.rem(c + 3, COLS)))[d]
        return pltpu.make_async_remote_copy(
            src_ref=packed.at[d],
            dst_ref=landed.at[d],
            send_sem=move_send.at[d],
            recv_sem=move_recv.at[d],
            device_id=target,
            device_id_type=MESH,
        )

    @pl.when(r < ROWS - 1)
    def _():
        move(0).start()

    @pl.when(r > 0)
    def _():
        move(1).start()

    move(2).start()
    move(3).start()

    def z_block(q, d):
        block = fields[q, :, x_here, :] if d == 0 else at_z[d - 1, q]
        return block.reshape(YR * 128, ZC)

    def z_terms(i, _):
        q = order(i)
        for d in range(1, COLS):
            to_z(d, q).wait_recv()
        wide = jnp.concatenate([z_block(q, d) for d in range(COLS)], axis=1)
        high, low = split(wide)
        result = mm(jnp.concatenate([high, low, high], axis=1), z_matrix[...])
        for e in range(COLS):
            along, curve = result[:, e * ZC : (e + 1) * ZC], result[:, NZ + e * ZC : NZ + (e + 1) * ZC]
            term = viscous[q] * curve - z_block(2, (COLS - e) % COLS) * along
            z_out[e, q] = term.reshape(YR, 128, ZC)
        for d in (1, 3, 2):
            from_z(d, q, c).start()
        return 0

    lax.fori_loop(0, 3, z_terms, 0)

    def y_terms(q, _):
        give(q).wait_recv()
        near = jnp.concatenate([at_y[q, :, x, :] for x in range(XB)], axis=1)
        far = jnp.concatenate([taken[q, :, x, :] for x in range(XB)], axis=1)
        high, low = split(jnp.concatenate([near, far], axis=0))
        result = mm(y_matrix[side], jnp.concatenate([high, low, high], axis=0))
        for x in range(XB):
            along, curve = result[:YH, x * ZC : (x + 1) * ZC], result[YH:, x * ZC : (x + 1) * ZC]
            y_out[q, :, x, :] = viscous[q] * curve - at_y[1, :, x, :] * along
        return 0

    lax.fori_loop(0, 4, y_terms, 0)
    back_y[:, :, pl.ds(pl.multiple_of(h * XB, XB), XB), :] = y_out[:, pl.ds(h * YR, YR)]

    def start_back_y(i, _):
        from_y(peer(i), h).start()
        return 0

    lax.fori_loop(1, HALF, start_back_y, 0)
    lax.fori_loop(3, 4, z_terms, 0)
    for q in range(4):
        tendency[q, :, x_here, :] += z_out[0, q]

    def wait_back_y(i, _):
        p = lax.rem(h + i, HALF)
        from_y(p, p).wait_recv()
        return 0

    lax.fori_loop(1, HALF, wait_back_y, 0)

    def add_y(q, _):
        tendency[q] += back_y[q]
        return 0

    lax.fori_loop(0, 4, add_y, 0)

    def finish(i, _):
        q = order(i)
        for d in (1, 3, 2):
            sender = lax.rem(c + COLS - d, COLS)
            from_z(d, q, sender).wait_recv()
            rows = pl.ds(pl.multiple_of(sender * 128, 128), 128)
            tendency[q, :, rows, :] += back_z[q, :, rows, :]
        return 0

    lax.fori_loop(0, 4, finish, 0)

    @pl.when(r > 0)
    def _():
        move(0).wait_recv()
        arrivals[:, 0, :] = landed[0, 0:6, :]

    @pl.when(r == 0)
    def _():
        arrivals[:, 0, :] = jnp.zeros((6, MIG), F32)

    @pl.when(r < ROWS - 1)
    def _():
        move(1).wait_recv()
        arrivals[:, 1, :] = landed[1, 0:6, :]

    @pl.when(r == ROWS - 1)
    def _():
        arrivals[:, 1, :] = jnp.zeros((6, MIG), F32)

    for d in (2, 3):
        move(d).wait_recv()
        arrivals[:, d, :] = landed[d, 0:6, :]

    @pl.when(r < ROWS - 1)
    def _():
        move(0).wait_send()

    @pl.when(r > 0)
    def _():
        move(1).wait_send()

    move(2).wait_send()
    move(3).wait_send()

    def sent_y(i, _):
        p = lax.rem(h + i, HALF)
        to_y(p, p).wait_send()
        from_y(p, p).wait_send()
        return 0

    lax.fori_loop(1, HALF, sent_y, 0)

    def sent_z(q, _):
        for d in range(1, COLS):
            to_z(d, q).wait_send()
            from_z(d, q, c).wait_send()
        give(q).wait_send()
        return 0

    lax.fori_loop(0, 4, sent_z, 0)


def on_device(fields, diffusivity, records, response_time, cell_index, counts, destination, slot):
    x_base, y_matrix, y_give, z_base = (jnp.asarray(m) for m in constants())
    vmem, smem = pl.BlockSpec(memory_space=pltpu.VMEM), pl.BlockSpec(memory_space=pltpu.SMEM)
    dma = pltpu.SemaphoreType.DMA
    tendency, kept, arrivals = pl.pallas_call(
        step_kernel,
        in_specs=[smem, smem] + [vmem] * 10,
        out_specs=[vmem] * 3,
        out_shape=[
            jax.ShapeDtypeStruct((4, YR, NX, ZC), F32),
            jax.ShapeDtypeStruct((6, PART), F32),
            jax.ShapeDtypeStruct((6, 4, MIG), F32),
        ],
        scratch_shapes=[
            pltpu.VMEM((4, YH, XB, ZC), F32),
            pltpu.VMEM((COLS - 1, 4, YR, 128, ZC), F32),
            pltpu.VMEM((4, YH, XB, ZC), F32),
            pltpu.VMEM((COLS, 4, YR, 128, ZC), F32),
            pltpu.VMEM((4, YR, NX, ZC), F32),
            pltpu.VMEM((4, YR, NX, ZC), F32),
            pltpu.VMEM((2 * NX, 3 * NX), BF16),
            pltpu.VMEM((3 * NZ, 2 * NZ), BF16),
            pltpu.VMEM((6 * ZC, CELLS), BF16),
            pltpu.VMEM((3, CELLS, ZC), F32),
            pltpu.VMEM((64, 128), F32),
            pltpu.VMEM((4, 8, MIG), F32),
            pltpu.VMEM((4, 8, MIG), F32),
            pltpu.VMEM((4, PAD, XB, ZC), F32),
            pltpu.VMEM((4, PAD, XB, ZC), F32),
            dma((HALF,)), dma((HALF,)), dma((HALF,)), dma((HALF,)),
            dma((COLS, 4)), dma((COLS, 4)), dma((COLS, 4)), dma((COLS, 4)),
            dma((4,)), dma((4,)), dma((4,)), dma((4,)),
        ],
        compiler_params=pltpu.CompilerParams(
            collective_id=0, has_side_effects=True, vmem_limit_bytes=VLIM << 20
        ),
        name="whole_step",
    )(
        counts, diffusivity, x_base, y_matrix, y_give, z_base, fields, records,
        response_time[None], cell_index[None], destination[None], slot[None],
    )
    return tendency, kept, arrivals.transpose(1, 0, 2)


def solution(mesh):
    both = ("row", "col")
    return jax.shard_map(
        on_device,
        mesh=mesh,
        in_specs=(
            P(None, "row", None, "col"),
            P(),
            P(None, both),
            P(both),
            P(both),
            P(both),
            P(both),
            P(both),
        ),
        out_specs=(P(None, "row", None, "col"), P(None, both), P(None, None, both)),
        check_vma=False,
    )
```

```python
import math

import jax
import jax.numpy as jnp
import numpy as np
from jax import lax
from jax.experimental import pallas as pl
from jax.experimental.pallas import tpu as pltpu
from jax.sharding import PartitionSpec as P

F32, BF16 = jnp.float32, jnp.bfloat16
NX, NY, NZ, YR, ZC = 512, 128, 512, 2, 128
PART, MIG = 8192, 256
ROWS, COLS = 64, 4
HALF = ROWS // 2
XB = NX // HALF
YH = NY // 2
RANK, PAD = 28, 32
CHUNK = 1024
EARLY = 5
VLIM = 46
MESH = pl.DeviceIdType.MESH
CELLS = YR * NX
STEP, COUPLING, STRETCH = 0.2, 0.5, 1.5


def periodic_compact(n):
    eye = np.eye(n)
    up, up2 = np.roll(eye, 1, 1), np.roll(eye, 2, 1)
    lhs = eye + (up + up.T) / 3.0
    rhs = (up - up.T) * 7.0 / 9.0 + (up2 - up2.T) / 36.0
    return np.linalg.solve(lhs, rhs)


def wall_compact(n):
    lhs, rhs = np.eye(n), np.zeros((n, n))
    for j in range(1, n - 1):
        near = j in (1, n - 2)
        lhs[j, j - 1] = lhs[j, j + 1] = 0.25 if near else 1.0 / 3.0
        rhs[j, j + 1] = 0.75 if near else 7.0 / 9.0
        rhs[j, j - 1] = -rhs[j, j + 1]
        if not near:
            rhs[j, j + 2], rhs[j, j - 2] = 1.0 / 36.0, -1.0 / 36.0
    lhs[0, 1] = lhs[n - 1, n - 2] = 2.0
    rhs[0, :3] = (-2.5, 2.0, 0.5)
    rhs[n - 1, n - 3 :] = (-0.5, -2.0, 2.5)
    eta = -1.0 + 2.0 * np.arange(n) / (n - 1)
    slope = STRETCH * (1.0 - np.tanh(STRETCH * eta) ** 2) / math.tanh(STRETCH)
    return np.linalg.solve(lhs, rhs) / slope[:, None]


def spectral(n):
    offset = np.arange(n)[:, None] - np.arange(n)[None, :]
    safe = np.where(offset == 0, 1, offset)
    value = math.pi / n * (1.0 - 2.0 * (offset % 2)) / np.tan(math.pi * safe / n)
    return np.where(offset == 0, 0.0, value)


def split_np(matrix):
    high = matrix.astype(np.float32).astype(BF16)
    low = (matrix - high.astype(np.float64)).astype(np.float32).astype(BF16)
    return high, low


def split(value):
    high = value.astype(BF16)
    return high, (value - high.astype(F32)).astype(BF16)


def constants():
    dx, dy, dz = periodic_compact(NX), wall_compact(NY), spectral(NZ)
    x_row = np.concatenate([dx[:128], (dx @ dx)[:128]], 0)
    z_t = np.concatenate([dz.T[:128], (dz @ dz).T[:128]], 0)
    x_high, x_low = split_np(x_row)
    z_high, z_low = split_np(z_t)
    halves = [np.concatenate([np.arange(b, b + 16) for b in range(16 * k, NY, 32)]) for k in range(2)]
    own, give = [], [None, None]
    for k, (mine, other) in enumerate((halves, halves[::-1])):
        both = np.concatenate([dy[mine], (dy @ dy)[mine]], 0)
        left, scale, right = np.linalg.svd(both[:, other])
        assert scale[RANK] < 1e-13 * scale[0]
        reached = np.zeros((2 * YH, PAD))
        reached[:, :RANK] = left[:, :RANK] * scale[:RANK]
        high, low = split_np(np.concatenate([both[:, mine], reached], 1))
        own.append(np.concatenate([high, high, low], 1))
        wanted = np.zeros((PAD, YH))
        wanted[:RANK] = right[:RANK]
        high, low = split_np(wanted)
        give[1 - k] = np.concatenate([high, high, low], 1)
    return np.stack([x_high, x_low]), np.stack(own), np.stack(give), np.stack([z_high, z_low])


def nt(a, b):
    return lax.dot_general(a, b, (((1,), (1,)), ((), ())), preferred_element_type=F32)


def mm(a, b):
    return jnp.dot(a, b, preferred_element_type=F32)


def expand(base, matrix, size, by_rows):
    for kind in range(2):
        for i in range(4):
            for j in range(4):
                at = ((j - i) if by_rows else (i + j)) % 4
                block = (slice(kind * 128, (kind + 1) * 128), slice(at * 128, (at + 1) * 128))
                for place, part in enumerate((0, 0, 1)):
                    tile = base[(part,) + block]
                    if by_rows:
                        matrix[pl.ds((kind * 4 + i) * 128, 128), pl.ds(place * size + j * 128, 128)] = tile
                    else:
                        matrix[pl.ds(place * size + i * 128, 128), pl.ds((kind * 4 + j) * 128, 128)] = tile


def step_kernel(
    *inputs_and_rest,
):
    counts, inputs, rest = inputs_and_rest[0], inputs_and_rest[1:12], inputs_and_rest[12:]
    (
        tendency, kept, arrivals,
        at_y, at_z, y_out, z_out, back_y, back_z, x_matrix, z_matrix, table, deposit, spilled, packed, landed,
        given, taken,
        viscous, x_base, y_matrix, y_give, z_base, fields, records, response, cell, dest, slot,
        y_send, y_recv, back_y_send, back_y_recv, z_send, z_recv, back_z_send, back_z_recv, move_send, move_recv,
        give_send, give_recv, loaded,
    ) = rest
    local = (viscous, x_base, y_matrix, y_give, z_base, fields, records, response, cell, dest, slot)
    loads = [pltpu.make_async_copy(a, b, loaded.at[i]) for i, (a, b) in enumerate(zip(inputs, local))]
    for load in loads[5:] + loads[:5]:
        load.start()
    r, c = lax.axis_index("row"), lax.axis_index("col")
    side = lax.rem(lax.div(r, 8), 2)
    h = lax.div(r, 16) * 8 + lax.rem(r, 8)
    partner = r + 8 - 16 * side

    def row_of(p):
        return lax.div(p, 8) * 16 + side * 8 + lax.rem(p, 8)

    x_here = pl.ds(pl.multiple_of(c * 128, 128), 128)

    barrier = pltpu.get_barrier_semaphore()

    def greet(i, _):
        target = (row_of(lax.rem(h + i, HALF)), c)
        pl.semaphore_signal(barrier, inc=1, device_id=target, device_id_type=MESH)
        return 0

    lax.fori_loop(1, HALF, greet, 0)
    for row in (partner, lax.rem(r + 1, ROWS), lax.rem(r + ROWS - 1, ROWS)):
        pl.semaphore_signal(barrier, inc=1, device_id=(row, c), device_id_type=MESH)
    for d in range(1, COLS):
        pl.semaphore_signal(barrier, inc=1, device_id=(r, lax.rem(c + d, COLS)), device_id_type=MESH)
    pl.semaphore_wait(barrier, HALF - 1 + 3 + COLS - 1)

    loads[5].wait()

    def peer(i):
        half = lax.div(i + 1, 2)
        return lax.rem(h + jnp.where(lax.rem(i, 2) == 1, half, HALF - half), HALF)

    def order(i):
        return jnp.where(i == 0, 2, jnp.where(i == 3, 3, i - 1))

    def give(q):
        return pltpu.make_async_remote_copy(
            src_ref=given.at[q, pl.ds(0, RANK)],
            dst_ref=taken.at[q, pl.ds(0, RANK)],
            send_sem=give_send.at[q],
            recv_sem=give_recv.at[q],
            device_id=(partner, c),
            device_id_type=MESH,
        )

    def to_y(p, from_row):
        return pltpu.make_async_remote_copy(
            src_ref=fields.at[:, :, pl.ds(pl.multiple_of(p * XB, XB), XB), :],
            dst_ref=at_y.at[:, pl.ds(from_row * YR, YR)],
            send_sem=y_send.at[p],
            recv_sem=y_recv.at[from_row],
            device_id=(row_of(p), c),
            device_id_type=MESH,
        )

    def from_y(p, from_row):
        return pltpu.make_async_remote_copy(
            src_ref=y_out.at[:, pl.ds(p * YR, YR)],
            dst_ref=back_y.at[:, :, pl.ds(pl.multiple_of(from_row * XB, XB), XB), :],
            send_sem=back_y_send.at[p],
            recv_sem=back_y_recv.at[from_row],
            device_id=(row_of(p), c),
            device_id_type=MESH,
        )

    def to_z(d, q):
        to = lax.rem(c + d, COLS)
        return pltpu.make_async_remote_copy(
            src_ref=fields.at[q, :, pl.ds(pl.multiple_of(to * 128, 128), 128), :],
            dst_ref=at_z.at[d - 1, q],
            send_sem=z_send.at[d, q],
            recv_sem=z_recv.at[d, q],
            device_id=(r, to),
            device_id_type=MESH,
        )

    def from_z(d, q, sender):
        return pltpu.make_async_remote_copy(
            src_ref=z_out.at[d, q],
            dst_ref=back_z.at[q, :, pl.ds(pl.multiple_of(sender * 128, 128), 128), :],
            send_sem=back_z_send.at[d, q],
            recv_sem=back_z_recv.at[d, q],
            device_id=(r, lax.rem(c + d, COLS)),
            device_id_type=MESH,
        )

    def start_z(i, _):
        for d in (1, 3, 2):
            to_z(d, order(i)).start()
        return 0

    def start_y(i, _):
        to_y(peer(i), h).start()
        return 0

    lax.fori_loop(0, 1, start_z, 0)
    lax.fori_loop(1, HALF, start_y, 0)
    lax.fori_loop(1, 3, start_z, 0)
    at_y[:, pl.ds(h * YR, YR)] = fields[:, :, pl.ds(pl.multiple_of(h * XB, XB), XB), :]
    taken[:, pl.ds(RANK, PAD - RANK)] = jnp.zeros((4, PAD - RANK, XB, ZC), F32)

    for load in loads[:5] + loads[6:]:
        load.wait()
    for a in range(3):
        high, low = split(fields[a].reshape(CELLS, ZC).T)
        table[pl.ds(a * ZC, ZC), :] = high
        table[pl.ds((3 + a) * ZC, ZC), :] = low
    deposit[...] = jnp.zeros_like(deposit)
    spilled[...] = jnp.zeros_like(spilled)
    expand(x_base, x_matrix, NX, True)
    expand(z_base, z_matrix, NZ, False)

    def particles(step, _):
        here = pl.ds(pl.multiple_of(step * CHUNK, CHUNK), CHUNK)
        index = cell[:, here]
        row, lane = index // ZC, index % ZC
        local = step * CHUNK + lax.broadcasted_iota(jnp.int32, (1, CHUNK), 1)
        live = local < counts[0]
        in_row = lax.broadcasted_iota(jnp.int32, (CELLS, CHUNK), 0) == row
        hot = jnp.where(in_row, 1.0, 0.0).astype(BF16)
        in_lane = lax.broadcasted_iota(jnp.int32, (ZC, CHUNK), 0) == lane
        picked = mm(table[...], hot)
        fluid = []
        for a in range(3):
            both = picked[a * ZC : (a + 1) * ZC] + picked[(3 + a) * ZC : (4 + a) * ZC]
            fluid.append(jnp.sum(jnp.where(in_lane, both, 0.0), axis=0, keepdims=True))
        fluid = jnp.concatenate(fluid, axis=0)
        speed = records[3:6, here]
        drag = (fluid - speed) / response[:, here]
        velocity = speed + STEP * drag
        moved = jnp.concatenate([records[0:3, here] + STEP * velocity, velocity], axis=0)
        to = dest[:, here]
        kept[:, here] = jnp.where(live & (to == 0), moved, 0.0)
        force = jnp.where(live, -COUPLING * drag, 0.0)
        spread = jnp.concatenate([jnp.where(in_lane, force[a : a + 1], 0.0) for a in range(3)], axis=0)
        high, low = split(spread)
        laid = nt(hot, high) + nt(hot, low)
        for a in range(3):
            deposit[a] += laid[:, a * ZC : (a + 1) * ZC]
        spot = slot[:, here]
        place = jnp.where(live & (to > 0), (to - 1) * 2 + spot // 128, 8)
        in_slot = lax.broadcasted_iota(jnp.int32, (128, CHUNK), 0) == spot % 128
        slot_hot = jnp.where(in_slot, 1.0, 0.0).astype(BF16)
        eight = jnp.concatenate([moved, jnp.zeros((2, CHUNK), F32)], axis=0)
        parts = jnp.concatenate([jnp.where(place == spot_at, eight, 0.0) for spot_at in range(8)], axis=0)
        high, low = split(parts)
        rest = (parts - high.astype(F32) - low.astype(F32)).astype(BF16)
        spilled[...] += nt(high, slot_hot) + nt(low, slot_hot) + nt(rest, slot_hot)
        return 0

    lax.fori_loop(0, EARLY, particles, 0)

    def wait_y(i, _):
        p = lax.rem(h + i, HALF)
        to_y(p, p).wait_recv()
        return 0

    lax.fori_loop(1, HALF, wait_y, 0)

    def wanted(q, _):
        wide = jnp.concatenate([at_y[q, :, x, :] for x in range(XB)], axis=1)
        high, low = split(wide)
        result = mm(y_give[side], jnp.concatenate([high, low, high], axis=0))
        for x in range(XB):
            given[q, :, x, :] = result[:, x * ZC : (x + 1) * ZC]
        return 0

    lax.fori_loop(0, 4, wanted, 0)
    for q in range(4):
        give(q).start()
    lax.fori_loop(3, 4, start_z, 0)

    lax.fori_loop(EARLY, PART // CHUNK, particles, 0)
    for d in range(4):
        for part in range(2):
            packed[d, :, pl.ds(part * 128, 128)] = spilled[pl.ds((2 * d + part) * 8, 8), :]

    def x_terms(q, _):
        value = jnp.concatenate([fields[q, y] for y in range(YR)], axis=1)
        high, low = split(value)
        result = mm(x_matrix[...], jnp.concatenate([high, low, high], axis=0))
        for y in range(YR):
            along, curve = result[:NX, y * ZC : (y + 1) * ZC], result[NX:, y * ZC : (y + 1) * ZC]
            tendency[q, y] = viscous[q] * curve - fields[0, y] * along
        return 0

    lax.fori_loop(0, 4, x_terms, 0)
    for a in range(3):
        for y in range(YR):
            tendency[a, y] += deposit[a, pl.ds(y * NX, NX), :]

    def move(d):
        target = ((lax.rem(r + 1, ROWS), c), (lax.rem(r + ROWS - 1, ROWS), c), (r, lax.rem(c + 1, COLS)), (r, lax.rem(c + 3, COLS)))[d]
        return pltpu.make_async_remote_copy(
            src_ref=packed.at[d],
            dst_ref=landed.at[d],
            send_sem=move_send.at[d],
            recv_sem=move_recv.at[d],
            device_id=target,
            device_id_type=MESH,
        )

    @pl.when(r < ROWS - 1)
    def _():
        move(0).start()

    @pl.when(r > 0)
    def _():
        move(1).start()

    move(2).start()
    move(3).start()

    def z_block(q, d):
        block = fields[q, :, x_here, :] if d == 0 else at_z[d - 1, q]
        return block.reshape(YR * 128, ZC)

    def z_terms(i, _):
        q = order(i)
        for d in range(1, COLS):
            to_z(d, q).wait_recv()
        wide = jnp.concatenate([z_block(q, d) for d in range(COLS)], axis=1)
        high, low = split(wide)
        result = mm(jnp.concatenate([high, low, high], axis=1), z_matrix[...])
        for e in range(COLS):
            along, curve = result[:, e * ZC : (e + 1) * ZC], result[:, NZ + e * ZC : NZ + (e + 1) * ZC]
            term = viscous[q] * curve - z_block(2, (COLS - e) % COLS) * along
            z_out[e, q] = term.reshape(YR, 128, ZC)
        for d in (1, 3, 2):
            from_z(d, q, c).start()
        return 0

    lax.fori_loop(0, 3, z_terms, 0)

    def y_terms(q, _):
        give(q).wait_recv()
        near = jnp.concatenate([at_y[q, :, x, :] for x in range(XB)], axis=1)
        far = jnp.concatenate([taken[q, :, x, :] for x in range(XB)], axis=1)
        high, low = split(jnp.concatenate([near, far], axis=0))
        result = mm(y_matrix[side], jnp.concatenate([high, low, high], axis=0))
        for x in range(XB):
            along, curve = result[:YH, x * ZC : (x + 1) * ZC], result[YH:, x * ZC : (x + 1) * ZC]
            y_out[q, :, x, :] = viscous[q] * curve - at_y[1, :, x, :] * along
        return 0

    lax.fori_loop(0, 4, y_terms, 0)
    back_y[:, :, pl.ds(pl.multiple_of(h * XB, XB), XB), :] = y_out[:, pl.ds(h * YR, YR)]

    def start_back_y(i, _):
        from_y(peer(i), h).start()
        return 0

    lax.fori_loop(1, HALF, start_back_y, 0)
    lax.fori_loop(3, 4, z_terms, 0)
    for q in range(4):
        tendency[q, :, x_here, :] += z_out[0, q]

    def wait_back_y(i, _):
        p = lax.rem(h + i, HALF)
        from_y(p, p).wait_recv()
        return 0

    lax.fori_loop(1, HALF, wait_back_y, 0)

    def add_y(q, _):
        tendency[q] += back_y[q]
        return 0

    lax.fori_loop(0, 4, add_y, 0)

    def finish(i, _):
        q = order(i)
        for d in (1, 3, 2):
            sender = lax.rem(c + COLS - d, COLS)
            from_z(d, q, sender).wait_recv()
            rows = pl.ds(pl.multiple_of(sender * 128, 128), 128)
            tendency[q, :, rows, :] += back_z[q, :, rows, :]
        return 0

    lax.fori_loop(0, 4, finish, 0)

    @pl.when(r > 0)
    def _():
        move(0).wait_recv()
        arrivals[:, 0, :] = landed[0, 0:6, :]

    @pl.when(r == 0)
    def _():
        arrivals[:, 0, :] = jnp.zeros((6, MIG), F32)

    @pl.when(r < ROWS - 1)
    def _():
        move(1).wait_recv()
        arrivals[:, 1, :] = landed[1, 0:6, :]

    @pl.when(r == ROWS - 1)
    def _():
        arrivals[:, 1, :] = jnp.zeros((6, MIG), F32)

    for d in (2, 3):
        move(d).wait_recv()
        arrivals[:, d, :] = landed[d, 0:6, :]

    @pl.when(r < ROWS - 1)
    def _():
        move(0).wait_send()

    @pl.when(r > 0)
    def _():
        move(1).wait_send()

    move(2).wait_send()
    move(3).wait_send()

    def sent_y(i, _):
        p = lax.rem(h + i, HALF)
        to_y(p, p).wait_send()
        from_y(p, p).wait_send()
        return 0

    lax.fori_loop(1, HALF, sent_y, 0)

    def sent_z(q, _):
        for d in range(1, COLS):
            to_z(d, q).wait_send()
            from_z(d, q, c).wait_send()
        give(q).wait_send()
        return 0

    lax.fori_loop(0, 4, sent_z, 0)


def on_device(fields, diffusivity, records, response_time, cell_index, counts, destination, slot):
    x_base, y_matrix, y_give, z_base = (jnp.asarray(m) for m in constants())
    vmem, hbm = pl.BlockSpec(memory_space=pltpu.VMEM), pl.BlockSpec(memory_space=pltpu.HBM)
    dma = pltpu.SemaphoreType.DMA
    tendency, kept, arrivals = pl.pallas_call(
        step_kernel,
        in_specs=[pl.BlockSpec(memory_space=pltpu.SMEM)] + [hbm] * 11,
        out_specs=[vmem] * 3,
        out_shape=[
            jax.ShapeDtypeStruct((4, YR, NX, ZC), F32),
            jax.ShapeDtypeStruct((6, PART), F32),
            jax.ShapeDtypeStruct((6, 4, MIG), F32),
        ],
        scratch_shapes=[
            pltpu.VMEM((4, YH, XB, ZC), F32),
            pltpu.VMEM((COLS - 1, 4, YR, 128, ZC), F32),
            pltpu.VMEM((4, YH, XB, ZC), F32),
            pltpu.VMEM((COLS, 4, YR, 128, ZC), F32),
            pltpu.VMEM((4, YR, NX, ZC), F32),
            pltpu.VMEM((4, YR, NX, ZC), F32),
            pltpu.VMEM((2 * NX, 3 * NX), BF16),
            pltpu.VMEM((3 * NZ, 2 * NZ), BF16),
            pltpu.VMEM((6 * ZC, CELLS), BF16),
            pltpu.VMEM((3, CELLS, ZC), F32),
            pltpu.VMEM((64, 128), F32),
            pltpu.VMEM((4, 8, MIG), F32),
            pltpu.VMEM((4, 8, MIG), F32),
            pltpu.VMEM((4, PAD, XB, ZC), F32),
            pltpu.VMEM((4, PAD, XB, ZC), F32),
            pltpu.SMEM((4,), F32),
            pltpu.VMEM((2, 256, NX), BF16),
            pltpu.VMEM((2, 2 * YH, 3 * (YH + PAD)), BF16),
            pltpu.VMEM((2, PAD, 3 * YH), BF16),
            pltpu.VMEM((2, 256, NZ), BF16),
            pltpu.VMEM((4, YR, NX, ZC), F32),
            pltpu.VMEM((6, PART), F32),
            pltpu.VMEM((1, PART), F32),
            pltpu.VMEM((1, PART), jnp.int32),
            pltpu.VMEM((1, PART), jnp.int32),
            pltpu.VMEM((1, PART), jnp.int32),
            dma((HALF,)), dma((HALF,)), dma((HALF,)), dma((HALF,)),
            dma((COLS, 4)), dma((COLS, 4)), dma((COLS, 4)), dma((COLS, 4)),
            dma((4,)), dma((4,)), dma((4,)), dma((4,)), dma((11,)),
        ],
        compiler_params=pltpu.CompilerParams(
            collective_id=0, has_side_effects=True, vmem_limit_bytes=VLIM << 20
        ),
        name="whole_step",
    )(counts, *(pltpu.with_memory_space_constraint(value, pltpu.HBM) for value in (
        diffusivity, x_base, y_matrix, y_give, z_base, fields, records,
        response_time[None], cell_index[None], destination[None], slot[None],
    )))
    return tendency, kept, arrivals.transpose(1, 0, 2)


def solution(mesh):
    both = ("row", "col")
    return jax.shard_map(
        on_device,
        mesh=mesh,
        in_specs=(
            P(None, "row", None, "col"),
            P(),
            P(None, both),
            P(both),
            P(both),
            P(both),
            P(both),
            P(both),
        ),
        out_specs=(P(None, "row", None, "col"), P(None, both), P(None, None, both)),
        check_vma=False,
    )
```

```python
import math

import jax
import jax.numpy as jnp
import numpy as np
from jax import lax
from jax.experimental import pallas as pl
from jax.experimental.pallas import tpu as pltpu
from jax.sharding import PartitionSpec as P

F32, BF16 = jnp.float32, jnp.bfloat16
NX, NY, NZ, YR, ZC = 512, 128, 512, 2, 128
PART, MIG = 8192, 256
ROWS, COLS = 64, 4
HALF = ROWS // 2
XB = NX // HALF
YH = NY // 2
RANK, PAD = 28, 32
CHUNK = 1024
EARLY = 5
VLIM = 46
MESH = pl.DeviceIdType.MESH
CELLS = YR * NX
STEP, COUPLING, STRETCH = 0.2, 0.5, 1.5


def periodic_compact(n):
    eye = np.eye(n)
    up, up2 = np.roll(eye, 1, 1), np.roll(eye, 2, 1)
    lhs = eye + (up + up.T) / 3.0
    rhs = (up - up.T) * 7.0 / 9.0 + (up2 - up2.T) / 36.0
    return np.linalg.solve(lhs, rhs)


def wall_compact(n):
    lhs, rhs = np.eye(n), np.zeros((n, n))
    for j in range(1, n - 1):
        near = j in (1, n - 2)
        lhs[j, j - 1] = lhs[j, j + 1] = 0.25 if near else 1.0 / 3.0
        rhs[j, j + 1] = 0.75 if near else 7.0 / 9.0
        rhs[j, j - 1] = -rhs[j, j + 1]
        if not near:
            rhs[j, j + 2], rhs[j, j - 2] = 1.0 / 36.0, -1.0 / 36.0
    lhs[0, 1] = lhs[n - 1, n - 2] = 2.0
    rhs[0, :3] = (-2.5, 2.0, 0.5)
    rhs[n - 1, n - 3 :] = (-0.5, -2.0, 2.5)
    eta = -1.0 + 2.0 * np.arange(n) / (n - 1)
    slope = STRETCH * (1.0 - np.tanh(STRETCH * eta) ** 2) / math.tanh(STRETCH)
    return np.linalg.solve(lhs, rhs) / slope[:, None]


def spectral(n):
    offset = np.arange(n)[:, None] - np.arange(n)[None, :]
    safe = np.where(offset == 0, 1, offset)
    value = math.pi / n * (1.0 - 2.0 * (offset % 2)) / np.tan(math.pi * safe / n)
    return np.where(offset == 0, 0.0, value)


def split_np(matrix):
    high = matrix.astype(np.float32).astype(BF16)
    low = (matrix - high.astype(np.float64)).astype(np.float32).astype(BF16)
    return high, low


def split(value):
    high = value.astype(BF16)
    return high, (value - high.astype(F32)).astype(BF16)


def constants():
    dx, dy, dz = periodic_compact(NX), wall_compact(NY), spectral(NZ)
    x_row = np.concatenate([dx[:128], (dx @ dx)[:128]], 0)
    z_t = np.concatenate([dz.T[:128], (dz @ dz).T[:128]], 0)
    x_high, x_low = split_np(x_row)
    z_high, z_low = split_np(z_t)
    halves = [np.concatenate([np.arange(b, b + 16) for b in range(16 * k, NY, 32)]) for k in range(2)]
    own, give = [], [None, None]
    for k, (mine, other) in enumerate((halves, halves[::-1])):
        both = np.concatenate([dy[mine], (dy @ dy)[mine]], 0)
        left, scale, right = np.linalg.svd(both[:, other])
        assert scale[RANK] < 1e-13 * scale[0]
        reached = np.zeros((2 * YH, PAD))
        reached[:, :RANK] = left[:, :RANK] * scale[:RANK]
        high, low = split_np(np.concatenate([both[:, mine], reached], 1))
        own.append(np.concatenate([high, high, low], 1))
        wanted = np.zeros((PAD, YH))
        wanted[:RANK] = right[:RANK]
        high, low = split_np(wanted)
        give[1 - k] = np.concatenate([high, high, low], 1)
    return np.stack([x_high, x_low]), np.stack(own), np.stack(give), np.stack([z_high, z_low])


def nt(a, b):
    return lax.dot_general(a, b, (((1,), (1,)), ((), ())), preferred_element_type=F32)


def mm(a, b):
    return jnp.dot(a, b, preferred_element_type=F32)


def expand(base, matrix, size, by_rows):
    for kind in range(2):
        for i in range(4):
            for j in range(4):
                at = ((j - i) if by_rows else (i + j)) % 4
                block = (slice(kind * 128, (kind + 1) * 128), slice(at * 128, (at + 1) * 128))
                for place, part in enumerate((0, 0, 1)):
                    tile = base[(part,) + block]
                    if by_rows:
                        matrix[pl.ds((kind * 4 + i) * 128, 128), pl.ds(place * size + j * 128, 128)] = tile
                    else:
                        matrix[pl.ds(place * size + i * 128, 128), pl.ds((kind * 4 + j) * 128, 128)] = tile


def step_kernel(
    *inputs_and_rest,
):
    counts, inputs, rest = inputs_and_rest[0], inputs_and_rest[1:12], inputs_and_rest[12:]
    (
        tendency, kept, arrivals,
        at_y, at_z, y_out, z_out, back_y, back_z, x_matrix, z_matrix, table, deposit, spilled, packed, landed,
        given, taken,
        viscous, x_base, y_matrix, y_give, z_base, fields, records, response, cell, dest, slot,
        y_send, y_recv, back_y_send, back_y_recv, z_send, z_recv, back_z_send, back_z_recv, move_send, move_recv,
        give_send, give_recv, loaded,
    ) = rest
    local = (viscous, x_base, y_matrix, y_give, z_base, fields, records, response, cell, dest, slot)
    loads = [pltpu.make_async_copy(a, b, loaded.at[i]) for i, (a, b) in enumerate(zip(inputs, local))]
    for load in loads[5:] + loads[:5]:
        load.start()
    r, c = lax.axis_index("row"), lax.axis_index("col")
    side = lax.rem(lax.div(r, 8), 2)
    h = lax.div(r, 16) * 8 + lax.rem(r, 8)
    partner = r + 8 - 16 * side

    def row_of(p):
        return lax.div(p, 8) * 16 + side * 8 + lax.rem(p, 8)

    x_here = pl.ds(pl.multiple_of(c * 128, 128), 128)

    barrier = pltpu.get_barrier_semaphore()

    def greet(i, _):
        target = (row_of(lax.rem(h + i, HALF)), c)
        pl.semaphore_signal(barrier, inc=1, device_id=target, device_id_type=MESH)
        return 0

    lax.fori_loop(1, HALF, greet, 0)
    for row in (partner, lax.rem(r + 1, ROWS), lax.rem(r + ROWS - 1, ROWS)):
        pl.semaphore_signal(barrier, inc=1, device_id=(row, c), device_id_type=MESH)
    for d in range(1, COLS):
        pl.semaphore_signal(barrier, inc=1, device_id=(r, lax.rem(c + d, COLS)), device_id_type=MESH)
    pl.semaphore_wait(barrier, HALF - 1 + 3 + COLS - 1)

    loads[5].wait()

    def peer(i):
        half = lax.div(i + 1, 2)
        return lax.rem(h + jnp.where(lax.rem(i, 2) == 1, half, HALF - half), HALF)

    def order(i):
        return jnp.where(i == 0, 2, jnp.where(i == 3, 3, i - 1))

    def give(q):
        return pltpu.make_async_remote_copy(
            src_ref=given.at[q, pl.ds(0, RANK)],
            dst_ref=taken.at[q, pl.ds(0, RANK)],
            send_sem=give_send.at[q],
            recv_sem=give_recv.at[q],
            device_id=(partner, c),
            device_id_type=MESH,
        )

    def to_y(p, from_row):
        return pltpu.make_async_remote_copy(
            src_ref=fields.at[:, :, pl.ds(pl.multiple_of(p * XB, XB), XB), :],
            dst_ref=at_y.at[:, pl.ds(from_row * YR, YR)],
            send_sem=y_send.at[p],
            recv_sem=y_recv.at[from_row],
            device_id=(row_of(p), c),
            device_id_type=MESH,
        )

    def from_y(p, from_row):
        return pltpu.make_async_remote_copy(
            src_ref=y_out.at[:, pl.ds(p * YR, YR)],
            dst_ref=back_y.at[:, :, pl.ds(pl.multiple_of(from_row * XB, XB), XB), :],
            send_sem=back_y_send.at[p],
            recv_sem=back_y_recv.at[from_row],
            device_id=(row_of(p), c),
            device_id_type=MESH,
        )

    def to_z(d, q):
        to = lax.rem(c + d, COLS)
        return pltpu.make_async_remote_copy(
            src_ref=fields.at[q, :, pl.ds(pl.multiple_of(to * 128, 128), 128), :],
            dst_ref=at_z.at[d - 1, q],
            send_sem=z_send.at[d, q],
            recv_sem=z_recv.at[d, q],
            device_id=(r, to),
            device_id_type=MESH,
        )

    def from_z(d, q, sender):
        return pltpu.make_async_remote_copy(
            src_ref=z_out.at[d, q],
            dst_ref=back_z.at[q, :, pl.ds(pl.multiple_of(sender * 128, 128), 128), :],
            send_sem=back_z_send.at[d, q],
            recv_sem=back_z_recv.at[d, q],
            device_id=(r, lax.rem(c + d, COLS)),
            device_id_type=MESH,
        )

    def start_z(i, _):
        for d in (2, 1, 3):
            to_z(d, order(i)).start()
        return 0

    def start_y(i, _):
        to_y(peer(i), h).start()
        return 0

    lax.fori_loop(0, 1, start_z, 0)
    lax.fori_loop(1, HALF, start_y, 0)
    lax.fori_loop(1, 3, start_z, 0)
    at_y[:, pl.ds(h * YR, YR)] = fields[:, :, pl.ds(pl.multiple_of(h * XB, XB), XB), :]
    taken[:, pl.ds(RANK, PAD - RANK)] = jnp.zeros((4, PAD - RANK, XB, ZC), F32)

    for load in loads[:5] + loads[6:]:
        load.wait()
    for a in range(3):
        high, low = split(fields[a].reshape(CELLS, ZC).T)
        table[pl.ds(a * ZC, ZC), :] = high
        table[pl.ds((3 + a) * ZC, ZC), :] = low
    deposit[...] = jnp.zeros_like(deposit)
    spilled[...] = jnp.zeros_like(spilled)
    expand(x_base, x_matrix, NX, True)
    expand(z_base, z_matrix, NZ, False)

    def particles(step, _):
        here = pl.ds(pl.multiple_of(step * CHUNK, CHUNK), CHUNK)
        index = cell[:, here]
        row, lane = index // ZC, index % ZC
        local = step * CHUNK + lax.broadcasted_iota(jnp.int32, (1, CHUNK), 1)
        live = local < counts[0]
        in_row = lax.broadcasted_iota(jnp.int32, (CELLS, CHUNK), 0) == row
        hot = jnp.where(in_row, 1.0, 0.0).astype(BF16)
        in_lane = lax.broadcasted_iota(jnp.int32, (ZC, CHUNK), 0) == lane
        picked = mm(table[...], hot)
        fluid = []
        for a in range(3):
            both = picked[a * ZC : (a + 1) * ZC] + picked[(3 + a) * ZC : (4 + a) * ZC]
            fluid.append(jnp.sum(jnp.where(in_lane, both, 0.0), axis=0, keepdims=True))
        fluid = jnp.concatenate(fluid, axis=0)
        speed = records[3:6, here]
        drag = (fluid - speed) / response[:, here]
        velocity = speed + STEP * drag
        moved = jnp.concatenate([records[0:3, here] + STEP * velocity, velocity], axis=0)
        to = dest[:, here]
        kept[:, here] = jnp.where(live & (to == 0), moved, 0.0)
        force = jnp.where(live, -COUPLING * drag, 0.0)
        spread = jnp.concatenate([jnp.where(in_lane, force[a : a + 1], 0.0) for a in range(3)], axis=0)
        high, low = split(spread)
        laid = nt(hot, high) + nt(hot, low)
        for a in range(3):
            deposit[a] += laid[:, a * ZC : (a + 1) * ZC]
        spot = slot[:, here]
        place = jnp.where(live & (to > 0), (to - 1) * 2 + spot // 128, 8)
        in_slot = lax.broadcasted_iota(jnp.int32, (128, CHUNK), 0) == spot % 128
        slot_hot = jnp.where(in_slot, 1.0, 0.0).astype(BF16)
        eight = jnp.concatenate([moved, jnp.zeros((2, CHUNK), F32)], axis=0)
        parts = jnp.concatenate([jnp.where(place == spot_at, eight, 0.0) for spot_at in range(8)], axis=0)
        high, low = split(parts)
        rest = (parts - high.astype(F32) - low.astype(F32)).astype(BF16)
        spilled[...] += nt(high, slot_hot) + nt(low, slot_hot) + nt(rest, slot_hot)
        return 0

    lax.fori_loop(0, EARLY, particles, 0)

    def wait_y(i, _):
        p = lax.rem(h + i, HALF)
        to_y(p, p).wait_recv()
        return 0

    lax.fori_loop(1, HALF, wait_y, 0)

    def wanted(q, _):
        wide = jnp.concatenate([at_y[q, :, x, :] for x in range(XB)], axis=1)
        high, low = split(wide)
        result = mm(y_give[side], jnp.concatenate([high, low, high], axis=0))
        for x in range(XB):
            given[q, :, x, :] = result[:, x * ZC : (x + 1) * ZC]
        return 0

    lax.fori_loop(0, 4, wanted, 0)
    for q in range(4):
        give(q).start()
    lax.fori_loop(3, 4, start_z, 0)

    lax.fori_loop(EARLY, PART // CHUNK, particles, 0)
    for d in range(4):
        for part in range(2):
            packed[d, :, pl.ds(part * 128, 128)] = spilled[pl.ds((2 * d + part) * 8, 8), :]

    def x_terms(q, _):
        value = jnp.concatenate([fields[q, y] for y in range(YR)], axis=1)
        high, low = split(value)
        result = mm(x_matrix[...], jnp.concatenate([high, low, high], axis=0))
        for y in range(YR):
            along, curve = result[:NX, y * ZC : (y + 1) * ZC], result[NX:, y * ZC : (y + 1) * ZC]
            tendency[q, y] = viscous[q] * curve - fields[0, y] * along
        return 0

    lax.fori_loop(0, 4, x_terms, 0)
    for a in range(3):
        for y in range(YR):
            tendency[a, y] += deposit[a, pl.ds(y * NX, NX), :]

    def move(d):
        target = ((lax.rem(r + 1, ROWS), c), (lax.rem(r + ROWS - 1, ROWS), c), (r, lax.rem(c + 1, COLS)), (r, lax.rem(c + 3, COLS)))[d]
        return pltpu.make_async_remote_copy(
            src_ref=packed.at[d],
            dst_ref=landed.at[d],
            send_sem=move_send.at[d],
            recv_sem=move_recv.at[d],
            device_id=target,
            device_id_type=MESH,
        )

    @pl.when(r < ROWS - 1)
    def _():
        move(0).start()

    @pl.when(r > 0)
    def _():
        move(1).start()

    move(2).start()
    move(3).start()

    def z_block(q, d):
        block = fields[q, :, x_here, :] if d == 0 else at_z[d - 1, q]
        return block.reshape(YR * 128, ZC)

    def z_terms(i, _):
        q = order(i)
        for d in range(1, COLS):
            to_z(d, q).wait_recv()
        wide = jnp.concatenate([z_block(q, d) for d in range(COLS)], axis=1)
        high, low = split(wide)
        result = mm(jnp.concatenate([high, low, high], axis=1), z_matrix[...])
        for e in range(COLS):
            along, curve = result[:, e * ZC : (e + 1) * ZC], result[:, NZ + e * ZC : NZ + (e + 1) * ZC]
            term = viscous[q] * curve - z_block(2, (COLS - e) % COLS) * along
            z_out[e, q] = term.reshape(YR, 128, ZC)
        for d in (2, 1, 3):
            from_z(d, q, c).start()
        return 0

    lax.fori_loop(0, 3, z_terms, 0)

    def y_terms(q, _):
        give(q).wait_recv()
        near = jnp.concatenate([at_y[q, :, x, :] for x in range(XB)], axis=1)
        far = jnp.concatenate([taken[q, :, x, :] for x in range(XB)], axis=1)
        high, low = split(jnp.concatenate([near, far], axis=0))
        result = mm(y_matrix[side], jnp.concatenate([high, low, high], axis=0))
        for x in range(XB):
            along, curve = result[:YH, x * ZC : (x + 1) * ZC], result[YH:, x * ZC : (x + 1) * ZC]
            y_out[q, :, x, :] = viscous[q] * curve - at_y[1, :, x, :] * along
        return 0

    lax.fori_loop(0, 4, y_terms, 0)
    back_y[:, :, pl.ds(pl.multiple_of(h * XB, XB), XB), :] = y_out[:, pl.ds(h * YR, YR)]

    def start_back_y(i, _):
        from_y(peer(i), h).start()
        return 0

    lax.fori_loop(1, HALF, start_back_y, 0)
    lax.fori_loop(3, 4, z_terms, 0)
    for q in range(4):
        tendency[q, :, x_here, :] += z_out[0, q]

    def wait_back_y(i, _):
        p = lax.rem(h + i, HALF)
        from_y(p, p).wait_recv()
        return 0

    lax.fori_loop(1, HALF, wait_back_y, 0)

    def add_y(q, _):
        tendency[q] += back_y[q]
        return 0

    lax.fori_loop(0, 4, add_y, 0)

    def finish(i, _):
        q = order(i)
        for d in (2, 1, 3):
            sender = lax.rem(c + COLS - d, COLS)
            from_z(d, q, sender).wait_recv()
            rows = pl.ds(pl.multiple_of(sender * 128, 128), 128)
            tendency[q, :, rows, :] += back_z[q, :, rows, :]
        return 0

    lax.fori_loop(0, 4, finish, 0)

    @pl.when(r > 0)
    def _():
        move(0).wait_recv()
        arrivals[:, 0, :] = landed[0, 0:6, :]

    @pl.when(r == 0)
    def _():
        arrivals[:, 0, :] = jnp.zeros((6, MIG), F32)

    @pl.when(r < ROWS - 1)
    def _():
        move(1).wait_recv()
        arrivals[:, 1, :] = landed[1, 0:6, :]

    @pl.when(r == ROWS - 1)
    def _():
        arrivals[:, 1, :] = jnp.zeros((6, MIG), F32)

    for d in (2, 3):
        move(d).wait_recv()
        arrivals[:, d, :] = landed[d, 0:6, :]

    @pl.when(r < ROWS - 1)
    def _():
        move(0).wait_send()

    @pl.when(r > 0)
    def _():
        move(1).wait_send()

    move(2).wait_send()
    move(3).wait_send()

    def sent_y(i, _):
        p = lax.rem(h + i, HALF)
        to_y(p, p).wait_send()
        from_y(p, p).wait_send()
        return 0

    lax.fori_loop(1, HALF, sent_y, 0)

    def sent_z(q, _):
        for d in range(1, COLS):
            to_z(d, q).wait_send()
            from_z(d, q, c).wait_send()
        give(q).wait_send()
        return 0

    lax.fori_loop(0, 4, sent_z, 0)


def hand_kernel(*refs):
    copies = [pltpu.make_async_copy(refs[i], refs[3 + i], refs[6].at[i]) for i in range(3)]
    for copy in copies:
        copy.start()
    for copy in copies:
        copy.wait()


def hand_over(*values):
    anywhere = pl.BlockSpec(memory_space=pl.ANY)
    return pl.pallas_call(
        hand_kernel,
        in_specs=[anywhere] * 3,
        out_specs=[anywhere] * 3,
        out_shape=[jax.ShapeDtypeStruct(value.shape, F32) for value in values],
        scratch_shapes=[pltpu.SemaphoreType.DMA((3,))],
        compiler_params=pltpu.CompilerParams(vmem_limit_bytes=1 << 20),
        name="hand_over",
    )(*values)


def on_device(fields, diffusivity, records, response_time, cell_index, counts, destination, slot):
    x_base, y_matrix, y_give, z_base = (jnp.asarray(m) for m in constants())
    vmem, hbm = pl.BlockSpec(memory_space=pltpu.VMEM), pl.BlockSpec(memory_space=pltpu.HBM)
    dma = pltpu.SemaphoreType.DMA
    tendency, kept, arrivals = pl.pallas_call(
        step_kernel,
        in_specs=[pl.BlockSpec(memory_space=pltpu.SMEM)] + [hbm] * 11,
        out_specs=[vmem] * 3,
        out_shape=[
            jax.ShapeDtypeStruct((4, YR, NX, ZC), F32),
            jax.ShapeDtypeStruct((6, PART), F32),
            jax.ShapeDtypeStruct((6, 4, MIG), F32),
        ],
        scratch_shapes=[
            pltpu.VMEM((4, YH, XB, ZC), F32),
            pltpu.VMEM((COLS - 1, 4, YR, 128, ZC), F32),
            pltpu.VMEM((4, YH, XB, ZC), F32),
            pltpu.VMEM((COLS, 4, YR, 128, ZC), F32),
            pltpu.VMEM((4, YR, NX, ZC), F32),
            pltpu.VMEM((4, YR, NX, ZC), F32),
            pltpu.VMEM((2 * NX, 3 * NX), BF16),
            pltpu.VMEM((3 * NZ, 2 * NZ), BF16),
            pltpu.VMEM((6 * ZC, CELLS), BF16),
            pltpu.VMEM((3, CELLS, ZC), F32),
            pltpu.VMEM((64, 128), F32),
            pltpu.VMEM((4, 8, MIG), F32),
            pltpu.VMEM((4, 8, MIG), F32),
            pltpu.VMEM((4, PAD, XB, ZC), F32),
            pltpu.VMEM((4, PAD, XB, ZC), F32),
            pltpu.SMEM((4,), F32),
            pltpu.VMEM((2, 256, NX), BF16),
            pltpu.VMEM((2, 2 * YH, 3 * (YH + PAD)), BF16),
            pltpu.VMEM((2, PAD, 3 * YH), BF16),
            pltpu.VMEM((2, 256, NZ), BF16),
            pltpu.VMEM((4, YR, NX, ZC), F32),
            pltpu.VMEM((6, PART), F32),
            pltpu.VMEM((1, PART), F32),
            pltpu.VMEM((1, PART), jnp.int32),
            pltpu.VMEM((1, PART), jnp.int32),
            pltpu.VMEM((1, PART), jnp.int32),
            dma((HALF,)), dma((HALF,)), dma((HALF,)), dma((HALF,)),
            dma((COLS, 4)), dma((COLS, 4)), dma((COLS, 4)), dma((COLS, 4)),
            dma((4,)), dma((4,)), dma((4,)), dma((4,)), dma((11,)),
        ],
        compiler_params=pltpu.CompilerParams(
            collective_id=0, has_side_effects=True, vmem_limit_bytes=VLIM << 20
        ),
        name="whole_step",
    )(counts, *(pltpu.with_memory_space_constraint(value, pltpu.HBM) for value in (
        diffusivity, x_base, y_matrix, y_give, z_base, fields, records,
        response_time[None], cell_index[None], destination[None], slot[None],
    )))
    tendency, kept, arrivals = hand_over(tendency, kept, arrivals)
    return tendency, kept, arrivals.transpose(1, 0, 2)


def solution(mesh):
    both = ("row", "col")
    return jax.shard_map(
        on_device,
        mesh=mesh,
        in_specs=(
            P(None, "row", None, "col"),
            P(),
            P(None, both),
            P(both),
            P(both),
            P(both),
            P(both),
            P(both),
        ),
        out_specs=(P(None, "row", None, "col"), P(None, both), P(None, None, both)),
        check_vma=False,
    )
```

```python
import math

import jax
import jax.numpy as jnp
import numpy as np
from jax import lax
from jax.experimental import pallas as pl
from jax.experimental.pallas import tpu as pltpu
from jax.sharding import PartitionSpec as P

F32, BF16 = jnp.float32, jnp.bfloat16
NX, NY, NZ, YR, ZC = 512, 128, 512, 2, 128
PART, MIG = 8192, 256
ROWS, COLS = 64, 4
HALF = ROWS // 2
XB = NX // HALF
YH = NY // 2
RANK, PAD = 28, 32
CHUNK = 1024
EARLY = 5
VLIM = 47
MESH = pl.DeviceIdType.MESH
CELLS = YR * NX
STEP, COUPLING, STRETCH = 0.2, 0.5, 1.5


def periodic_compact(n):
    eye = np.eye(n)
    up, up2 = np.roll(eye, 1, 1), np.roll(eye, 2, 1)
    lhs = eye + (up + up.T) / 3.0
    rhs = (up - up.T) * 7.0 / 9.0 + (up2 - up2.T) / 36.0
    return np.linalg.solve(lhs, rhs)


def wall_compact(n):
    lhs, rhs = np.eye(n), np.zeros((n, n))
    for j in range(1, n - 1):
        near = j in (1, n - 2)
        lhs[j, j - 1] = lhs[j, j + 1] = 0.25 if near else 1.0 / 3.0
        rhs[j, j + 1] = 0.75 if near else 7.0 / 9.0
        rhs[j, j - 1] = -rhs[j, j + 1]
        if not near:
            rhs[j, j + 2], rhs[j, j - 2] = 1.0 / 36.0, -1.0 / 36.0
    lhs[0, 1] = lhs[n - 1, n - 2] = 2.0
    rhs[0, :3] = (-2.5, 2.0, 0.5)
    rhs[n - 1, n - 3 :] = (-0.5, -2.0, 2.5)
    eta = -1.0 + 2.0 * np.arange(n) / (n - 1)
    slope = STRETCH * (1.0 - np.tanh(STRETCH * eta) ** 2) / math.tanh(STRETCH)
    return np.linalg.solve(lhs, rhs) / slope[:, None]


def spectral(n):
    offset = np.arange(n)[:, None] - np.arange(n)[None, :]
    safe = np.where(offset == 0, 1, offset)
    value = math.pi / n * (1.0 - 2.0 * (offset % 2)) / np.tan(math.pi * safe / n)
    return np.where(offset == 0, 0.0, value)


def split_np(matrix):
    parts = []
    for _ in range(3):
        parts.append(matrix.astype(np.float32).astype(BF16))
        matrix = matrix - parts[-1].astype(np.float64)
    return parts


def split(value):
    parts = []
    for _ in range(3):
        parts.append(value.astype(BF16))
        value = value - parts[-1].astype(F32)
    return parts


def six(matrix, value):
    high, middle, low = split(value)
    size = value.shape[0]
    result = mm(matrix[:, :size], low) + mm(matrix[:, : 2 * size], jnp.concatenate([middle] * 2, axis=0))
    return result + mm(matrix[:, : 3 * size], jnp.concatenate([high] * 3, axis=0))


def six_right(value, matrix):
    high, middle, low = split(value)
    size = value.shape[1]
    result = mm(low, matrix[:size]) + mm(jnp.concatenate([middle] * 2, axis=1), matrix[: 2 * size])
    return result + mm(jnp.concatenate([high] * 3, axis=1), matrix[: 3 * size])


def constants():
    dx, dy, dz = periodic_compact(NX), wall_compact(NY), spectral(NZ)
    x_row = np.concatenate([dx[:128], (dx @ dx)[:128]], 0)
    z_t = np.concatenate([dz.T[:128], (dz @ dz).T[:128]], 0)
    halves = [np.concatenate([np.arange(b, b + 16) for b in range(16 * k, NY, 32)]) for k in range(2)]
    own, give = [], [None, None]
    for k, (mine, other) in enumerate((halves, halves[::-1])):
        both = np.concatenate([dy[mine], (dy @ dy)[mine]], 0)
        left, scale, right = np.linalg.svd(both[:, other])
        assert scale[RANK] < 1e-13 * scale[0]
        reached = np.zeros((2 * YH, PAD))
        reached[:, :RANK] = left[:, :RANK] * scale[:RANK]
        own.append(np.concatenate(split_np(np.concatenate([both[:, mine], reached], 1)), 1))
        wanted = np.zeros((PAD, YH))
        wanted[:RANK] = right[:RANK]
        give[1 - k] = np.concatenate(split_np(wanted), 1)
    return np.stack(split_np(x_row)), np.stack(own), np.stack(give), np.stack(split_np(z_t))


def nt(a, b):
    return lax.dot_general(a, b, (((1,), (1,)), ((), ())), preferred_element_type=F32)


def mm(a, b):
    return jnp.dot(a, b, preferred_element_type=F32)


def expand(base, matrix, size, by_rows):
    for kind in range(2):
        for i in range(4):
            for j in range(4):
                at = ((j - i) if by_rows else (i + j)) % 4
                block = (slice(kind * 128, (kind + 1) * 128), slice(at * 128, (at + 1) * 128))
                for place, part in enumerate((0, 1, 2)):
                    tile = base[(part,) + block]
                    if by_rows:
                        matrix[pl.ds((kind * 4 + i) * 128, 128), pl.ds(place * size + j * 128, 128)] = tile
                    else:
                        matrix[pl.ds(place * size + i * 128, 128), pl.ds((kind * 4 + j) * 128, 128)] = tile


def step_kernel(
    *inputs_and_rest,
):
    counts, inputs, rest = inputs_and_rest[0], inputs_and_rest[1:12], inputs_and_rest[12:]
    (
        tendency, kept, arrivals,
        at_y, at_z, y_out, z_out, back_y, back_z, x_matrix, z_matrix, table, deposit, spilled, packed, landed,
        given, taken,
        viscous, x_base, y_matrix, y_give, z_base, fields, records, response, cell, dest, slot,
        y_send, y_recv, back_y_send, back_y_recv, z_send, z_recv, back_z_send, back_z_recv, move_send, move_recv,
        give_send, give_recv, loaded,
    ) = rest
    local = (viscous, x_base, y_matrix, y_give, z_base, fields, records, response, cell, dest, slot)
    loads = [pltpu.make_async_copy(a, b, loaded.at[i]) for i, (a, b) in enumerate(zip(inputs, local))]
    for load in loads[5:] + loads[:5]:
        load.start()
    r, c = lax.axis_index("row"), lax.axis_index("col")
    side = lax.rem(lax.div(r, 8), 2)
    h = lax.div(r, 16) * 8 + lax.rem(r, 8)
    partner = r + 8 - 16 * side

    def row_of(p):
        return lax.div(p, 8) * 16 + side * 8 + lax.rem(p, 8)

    x_here = pl.ds(pl.multiple_of(c * 128, 128), 128)

    barrier = pltpu.get_barrier_semaphore()

    def greet(i, _):
        target = (row_of(lax.rem(h + i, HALF)), c)
        pl.semaphore_signal(barrier, inc=1, device_id=target, device_id_type=MESH)
        return 0

    lax.fori_loop(1, HALF, greet, 0)
    for row in (partner, lax.rem(r + 1, ROWS), lax.rem(r + ROWS - 1, ROWS)):
        pl.semaphore_signal(barrier, inc=1, device_id=(row, c), device_id_type=MESH)
    for d in range(1, COLS):
        pl.semaphore_signal(barrier, inc=1, device_id=(r, lax.rem(c + d, COLS)), device_id_type=MESH)
    pl.semaphore_wait(barrier, HALF - 1 + 3 + COLS - 1)

    loads[5].wait()

    def peer(i):
        half = lax.div(i + 1, 2)
        return lax.rem(h + jnp.where(lax.rem(i, 2) == 1, half, HALF - half), HALF)

    def order(i):
        return jnp.where(i == 0, 2, jnp.where(i == 3, 3, i - 1))

    def give(q):
        return pltpu.make_async_remote_copy(
            src_ref=given.at[q, pl.ds(0, RANK)],
            dst_ref=taken.at[q, pl.ds(0, RANK)],
            send_sem=give_send.at[q],
            recv_sem=give_recv.at[q],
            device_id=(partner, c),
            device_id_type=MESH,
        )

    def to_y(p, from_row):
        return pltpu.make_async_remote_copy(
            src_ref=fields.at[:, :, pl.ds(pl.multiple_of(p * XB, XB), XB), :],
            dst_ref=at_y.at[:, pl.ds(from_row * YR, YR)],
            send_sem=y_send.at[p],
            recv_sem=y_recv.at[from_row],
            device_id=(row_of(p), c),
            device_id_type=MESH,
        )

    def from_y(p, from_row):
        return pltpu.make_async_remote_copy(
            src_ref=y_out.at[:, pl.ds(p * YR, YR)],
            dst_ref=back_y.at[:, :, pl.ds(pl.multiple_of(from_row * XB, XB), XB), :],
            send_sem=back_y_send.at[p],
            recv_sem=back_y_recv.at[from_row],
            device_id=(row_of(p), c),
            device_id_type=MESH,
        )

    def to_z(d, q):
        to = lax.rem(c + d, COLS)
        return pltpu.make_async_remote_copy(
            src_ref=fields.at[q, :, pl.ds(pl.multiple_of(to * 128, 128), 128), :],
            dst_ref=at_z.at[d - 1, q],
            send_sem=z_send.at[d, q],
            recv_sem=z_recv.at[d, q],
            device_id=(r, to),
            device_id_type=MESH,
        )

    def from_z(d, q, sender):
        return pltpu.make_async_remote_copy(
            src_ref=z_out.at[d, q],
            dst_ref=back_z.at[q, :, pl.ds(pl.multiple_of(sender * 128, 128), 128), :],
            send_sem=back_z_send.at[d, q],
            recv_sem=back_z_recv.at[d, q],
            device_id=(r, lax.rem(c + d, COLS)),
            device_id_type=MESH,
        )

    def start_z(i, _):
        for d in (2, 1, 3):
            to_z(d, order(i)).start()
        return 0

    def start_y(i, _):
        to_y(peer(i), h).start()
        return 0

    lax.fori_loop(0, 1, start_z, 0)
    lax.fori_loop(1, HALF, start_y, 0)
    lax.fori_loop(1, 3, start_z, 0)
    at_y[:, pl.ds(h * YR, YR)] = fields[:, :, pl.ds(pl.multiple_of(h * XB, XB), XB), :]
    taken[:, pl.ds(RANK, PAD - RANK)] = jnp.zeros((4, PAD - RANK, XB, ZC), F32)

    for load in loads[:5] + loads[6:]:
        load.wait()
    for a in range(3):
        for i, part in enumerate(split(fields[a].reshape(CELLS, ZC).T)):
            table[pl.ds((3 * i + a) * ZC, ZC), :] = part
    deposit[...] = jnp.zeros_like(deposit)
    spilled[...] = jnp.zeros_like(spilled)
    expand(x_base, x_matrix, NX, True)
    expand(z_base, z_matrix, NZ, False)

    def particles(step, _):
        here = pl.ds(pl.multiple_of(step * CHUNK, CHUNK), CHUNK)
        index = cell[:, here]
        row, lane = index // ZC, index % ZC
        local = step * CHUNK + lax.broadcasted_iota(jnp.int32, (1, CHUNK), 1)
        live = local < counts[0]
        in_row = lax.broadcasted_iota(jnp.int32, (CELLS, CHUNK), 0) == row
        hot = jnp.where(in_row, 1.0, 0.0).astype(BF16)
        in_lane = lax.broadcasted_iota(jnp.int32, (ZC, CHUNK), 0) == lane
        picked = mm(table[...], hot)
        fluid = []
        for a in range(3):
            both = picked[(6 + a) * ZC : (7 + a) * ZC] + picked[(3 + a) * ZC : (4 + a) * ZC]
            both = picked[a * ZC : (a + 1) * ZC] + both
            fluid.append(jnp.sum(jnp.where(in_lane, both, 0.0), axis=0, keepdims=True))
        fluid = jnp.concatenate(fluid, axis=0)
        speed = records[3:6, here]
        drag = (fluid - speed) / response[:, here]
        velocity = speed + STEP * drag
        moved = jnp.concatenate([records[0:3, here] + STEP * velocity, velocity], axis=0)
        to = dest[:, here]
        kept[:, here] = jnp.where(live & (to == 0), moved, 0.0)
        force = jnp.where(live, -COUPLING * drag, 0.0)
        spread = jnp.concatenate([jnp.where(in_lane, force[a : a + 1], 0.0) for a in range(3)], axis=0)
        high, middle, low = split(spread)
        laid = nt(hot, low) + nt(hot, middle) + nt(hot, high)
        for a in range(3):
            deposit[a] += laid[:, a * ZC : (a + 1) * ZC]
        spot = slot[:, here]
        place = jnp.where(live & (to > 0), (to - 1) * 2 + spot // 128, 8)
        in_slot = lax.broadcasted_iota(jnp.int32, (128, CHUNK), 0) == spot % 128
        slot_hot = jnp.where(in_slot, 1.0, 0.0).astype(BF16)
        eight = jnp.concatenate([moved, jnp.zeros((2, CHUNK), F32)], axis=0)
        parts = jnp.concatenate([jnp.where(place == spot_at, eight, 0.0) for spot_at in range(8)], axis=0)
        high, middle, low = split(parts)
        spilled[...] += nt(low, slot_hot) + nt(middle, slot_hot) + nt(high, slot_hot)
        return 0

    lax.fori_loop(0, EARLY, particles, 0)

    def wait_y(i, _):
        p = lax.rem(h + i, HALF)
        to_y(p, p).wait_recv()
        return 0

    lax.fori_loop(1, HALF, wait_y, 0)

    def wanted(q, _):
        wide = jnp.concatenate([at_y[q, :, x, :] for x in range(XB)], axis=1)
        result = six(y_give[side], wide)
        for x in range(XB):
            given[q, :, x, :] = result[:, x * ZC : (x + 1) * ZC]
        return 0

    lax.fori_loop(0, 4, wanted, 0)
    for q in range(4):
        give(q).start()
    lax.fori_loop(3, 4, start_z, 0)

    lax.fori_loop(EARLY, PART // CHUNK, particles, 0)
    for d in range(4):
        for part in range(2):
            packed[d, :, pl.ds(part * 128, 128)] = spilled[pl.ds((2 * d + part) * 8, 8), :]

    def x_terms(q, _):
        value = jnp.concatenate([fields[q, y] for y in range(YR)], axis=1)
        result = six(x_matrix, value)
        for y in range(YR):
            along, curve = result[:NX, y * ZC : (y + 1) * ZC], result[NX:, y * ZC : (y + 1) * ZC]
            tendency[q, y] = viscous[q] * curve - fields[0, y] * along
        return 0


    def move(d):
        target = ((lax.rem(r + 1, ROWS), c), (lax.rem(r + ROWS - 1, ROWS), c), (r, lax.rem(c + 1, COLS)), (r, lax.rem(c + 3, COLS)))[d]
        return pltpu.make_async_remote_copy(
            src_ref=packed.at[d],
            dst_ref=landed.at[d],
            send_sem=move_send.at[d],
            recv_sem=move_recv.at[d],
            device_id=target,
            device_id_type=MESH,
        )

    @pl.when(r < ROWS - 1)
    def _():
        move(0).start()

    @pl.when(r > 0)
    def _():
        move(1).start()

    move(2).start()
    move(3).start()

    def z_block(q, d):
        block = fields[q, :, x_here, :] if d == 0 else at_z[d - 1, q]
        return block.reshape(YR * 128, ZC)

    def z_terms(i, _):
        q = order(i)
        for d in range(1, COLS):
            to_z(d, q).wait_recv()
        wide = jnp.concatenate([z_block(q, d) for d in range(COLS)], axis=1)
        result = six_right(wide, z_matrix)
        for e in range(COLS):
            along, curve = result[:, e * ZC : (e + 1) * ZC], result[:, NZ + e * ZC : NZ + (e + 1) * ZC]
            term = viscous[q] * curve - z_block(2, (COLS - e) % COLS) * along
            z_out[e, q] = term.reshape(YR, 128, ZC)
        for d in (2, 1, 3):
            from_z(d, q, c).start()
        return 0

    lax.fori_loop(0, 3, z_terms, 0)

    def y_terms(q, _):
        give(q).wait_recv()
        near = jnp.concatenate([at_y[q, :, x, :] for x in range(XB)], axis=1)
        far = jnp.concatenate([taken[q, :, x, :] for x in range(XB)], axis=1)
        result = six(y_matrix[side], jnp.concatenate([near, far], axis=0))
        for x in range(XB):
            along, curve = result[:YH, x * ZC : (x + 1) * ZC], result[YH:, x * ZC : (x + 1) * ZC]
            y_out[q, :, x, :] = viscous[q] * curve - at_y[1, :, x, :] * along
        return 0

    lax.fori_loop(0, 4, y_terms, 0)
    back_y[:, :, pl.ds(pl.multiple_of(h * XB, XB), XB), :] = y_out[:, pl.ds(h * YR, YR)]

    def start_back_y(i, _):
        from_y(peer(i), h).start()
        return 0

    lax.fori_loop(1, HALF, start_back_y, 0)
    lax.fori_loop(3, 4, z_terms, 0)
    lax.fori_loop(0, 4, x_terms, 0)
    for a in range(3):
        for y in range(YR):
            tendency[a, y] += deposit[a, pl.ds(y * NX, NX), :]
    for q in range(4):
        tendency[q, :, x_here, :] += z_out[0, q]

    def wait_back_y(i, _):
        p = lax.rem(h + i, HALF)
        from_y(p, p).wait_recv()
        return 0

    lax.fori_loop(1, HALF, wait_back_y, 0)

    def add_y(q, _):
        tendency[q] += back_y[q]
        return 0

    lax.fori_loop(0, 4, add_y, 0)

    def finish(i, _):
        q = order(i)
        for d in (2, 1, 3):
            sender = lax.rem(c + COLS - d, COLS)
            from_z(d, q, sender).wait_recv()
            rows = pl.ds(pl.multiple_of(sender * 128, 128), 128)
            tendency[q, :, rows, :] += back_z[q, :, rows, :]
        return 0

    lax.fori_loop(0, 4, finish, 0)

    @pl.when(r > 0)
    def _():
        move(0).wait_recv()
        arrivals[:, 0, :] = landed[0, 0:6, :]

    @pl.when(r == 0)
    def _():
        arrivals[:, 0, :] = jnp.zeros((6, MIG), F32)

    @pl.when(r < ROWS - 1)
    def _():
        move(1).wait_recv()
        arrivals[:, 1, :] = landed[1, 0:6, :]

    @pl.when(r == ROWS - 1)
    def _():
        arrivals[:, 1, :] = jnp.zeros((6, MIG), F32)

    for d in (2, 3):
        move(d).wait_recv()
        arrivals[:, d, :] = landed[d, 0:6, :]

    @pl.when(r < ROWS - 1)
    def _():
        move(0).wait_send()

    @pl.when(r > 0)
    def _():
        move(1).wait_send()

    move(2).wait_send()
    move(3).wait_send()

    def sent_y(i, _):
        p = lax.rem(h + i, HALF)
        to_y(p, p).wait_send()
        from_y(p, p).wait_send()
        return 0

    lax.fori_loop(1, HALF, sent_y, 0)

    def sent_z(q, _):
        for d in range(1, COLS):
            to_z(d, q).wait_send()
            from_z(d, q, c).wait_send()
        give(q).wait_send()
        return 0

    lax.fori_loop(0, 4, sent_z, 0)


def hand_kernel(*refs):
    copies = [pltpu.make_async_copy(refs[i], refs[3 + i], refs[6].at[i]) for i in range(3)]
    for copy in copies:
        copy.start()
    for copy in copies:
        copy.wait()


def hand_over(*values):
    anywhere = pl.BlockSpec(memory_space=pl.ANY)
    return pl.pallas_call(
        hand_kernel,
        in_specs=[anywhere] * 3,
        out_specs=[anywhere] * 3,
        out_shape=[jax.ShapeDtypeStruct(value.shape, F32) for value in values],
        scratch_shapes=[pltpu.SemaphoreType.DMA((3,))],
        compiler_params=pltpu.CompilerParams(vmem_limit_bytes=1 << 20),
        name="hand_over",
    )(*values)


def on_device(fields, diffusivity, records, response_time, cell_index, counts, destination, slot):
    x_base, y_matrix, y_give, z_base = (jnp.asarray(m) for m in constants())
    vmem, hbm = pl.BlockSpec(memory_space=pltpu.VMEM), pl.BlockSpec(memory_space=pltpu.HBM)
    dma = pltpu.SemaphoreType.DMA
    tendency, kept, arrivals = pl.pallas_call(
        step_kernel,
        in_specs=[pl.BlockSpec(memory_space=pltpu.SMEM)] + [hbm] * 11,
        out_specs=[vmem] * 3,
        out_shape=[
            jax.ShapeDtypeStruct((4, YR, NX, ZC), F32),
            jax.ShapeDtypeStruct((6, PART), F32),
            jax.ShapeDtypeStruct((6, 4, MIG), F32),
        ],
        scratch_shapes=[
            pltpu.VMEM((4, YH, XB, ZC), F32),
            pltpu.VMEM((COLS - 1, 4, YR, 128, ZC), F32),
            pltpu.VMEM((4, YH, XB, ZC), F32),
            pltpu.VMEM((COLS, 4, YR, 128, ZC), F32),
            pltpu.VMEM((4, YR, NX, ZC), F32),
            pltpu.VMEM((4, YR, NX, ZC), F32),
            pltpu.VMEM((2 * NX, 3 * NX), BF16),
            pltpu.VMEM((3 * NZ, 2 * NZ), BF16),
            pltpu.VMEM((9 * ZC, CELLS), BF16),
            pltpu.VMEM((3, CELLS, ZC), F32),
            pltpu.VMEM((64, 128), F32),
            pltpu.VMEM((4, 8, MIG), F32),
            pltpu.VMEM((4, 8, MIG), F32),
            pltpu.VMEM((4, PAD, XB, ZC), F32),
            pltpu.VMEM((4, PAD, XB, ZC), F32),
            pltpu.SMEM((4,), F32),
            pltpu.VMEM((3, 256, NX), BF16),
            pltpu.VMEM((2, 2 * YH, 3 * (YH + PAD)), BF16),
            pltpu.VMEM((2, PAD, 3 * YH), BF16),
            pltpu.VMEM((3, 256, NZ), BF16),
            pltpu.VMEM((4, YR, NX, ZC), F32),
            pltpu.VMEM((6, PART), F32),
            pltpu.VMEM((1, PART), F32),
            pltpu.VMEM((1, PART), jnp.int32),
            pltpu.VMEM((1, PART), jnp.int32),
            pltpu.VMEM((1, PART), jnp.int32),
            dma((HALF,)), dma((HALF,)), dma((HALF,)), dma((HALF,)),
            dma((COLS, 4)), dma((COLS, 4)), dma((COLS, 4)), dma((COLS, 4)),
            dma((4,)), dma((4,)), dma((4,)), dma((4,)), dma((11,)),
        ],
        compiler_params=pltpu.CompilerParams(
            collective_id=0, has_side_effects=True, vmem_limit_bytes=VLIM << 20
        ),
        name="whole_step",
    )(counts, *(pltpu.with_memory_space_constraint(value, pltpu.HBM) for value in (
        diffusivity, x_base, y_matrix, y_give, z_base, fields, records,
        response_time[None], cell_index[None], destination[None], slot[None],
    )))
    tendency, kept, arrivals = hand_over(tendency, kept, arrivals)
    return tendency, kept, arrivals.transpose(1, 0, 2)


def solution(mesh):
    both = ("row", "col")
    return jax.shard_map(
        on_device,
        mesh=mesh,
        in_specs=(
            P(None, "row", None, "col"),
            P(),
            P(None, both),
            P(both),
            P(both),
            P(both),
            P(both),
            P(both),
        ),
        out_specs=(P(None, "row", None, "col"), P(None, both), P(None, None, both)),
        check_vma=False,
    )
```
